128 devices in a mesh: role: 2 (over x_hi), shard: 16 (over z, y), rep: 4 (over x_lo, core).
Axes of the slice: x: 4 (x_hi: 2, x_lo: 2; x = x_hi * 2 + x_lo), y: 4, z: 4, core: 2. Of those that a mesh axis runs over, the one named last changes fastest.
Arguments:
- qkv_versions: bfloat16 [2, 5120, 7168], P('role', 'rep', 'shard'), may hold values from -0.078125 to 0.078125
- qkv_bias: bfloat16 [2, 7168], P('role'), may hold values from -3 to 3
- o_versions: bfloat16 [2, 5120, 5120], P('role', 'rep', 'shard'), may hold values from -0.078125 to 0.078125
- norm_gain: bfloat16 [2, 5120], P('role'), may hold values from 0.5 to 1.5
- hidden: bfloat16 [2, 1024, 4, 5120], P('role', ('shard', 'rep')), may hold values from -6 to 6
- cache_keys: bfloat16 [2, 1024, 128, 1024], P('role', ('shard', 'rep')), may hold values from -220 to 220
- cache_values: bfloat16 [2, 1024, 128, 1024], P('role', ('shard', 'rep')), may hold values from -6 to 6
- lengths: int32 [2, 1024], P('role', ('shard', 'rep')), may hold values from 2 to 128, as said below
Outputs:
- layer_out: bfloat16 [2, 1024, 4, 5120], P('role', ('shard', 'rep'))
- new_qkv: bfloat16 [2, 5120, 7168], P('role', 'rep', 'shard')
- new_o: bfloat16 [2, 5120, 5120], P('role', 'rep', 'shard')
The draws below stay inside these ranges and needn't reach their ends.
Inputs may be any that keep to these rules, and one draw needn't show every extreme that they name: `lengths`: in every aligned group of 16 rows of a role at least one row has all 128 positions live.
All inputs are finite; a program needn't handle non-finite values.
Results may differ from the reference program's by a relative error of at most 0.0065.
The reference program's roundings to bfloat16 on the way count: a program that leaves them out, or rounds other values in their place, can miss the bound.
Values may be sent and summed in bfloat16 or wider, within the bound.
No kernel may reach another device: no remote copies, remote signals or barrier semaphores. Data moves between devices by JAX's collectives and lax.ppermute only.
A program may use at most 128 MiB of HBM per device.

```python
import math
import jax
import jax.numpy as jnp
from jax import lax

FACTOR_A = 40
FACTOR_B = 128
D = 5120
HEADS = 40
KV_HEADS = 8
HEAD_DIM = 128
QDIM = 5120
KVD = 1024
QKV = 7168
ROWS_DEV = 16
CACHE = 128
STEPS = 4
ROWS = 1024
N_ROLE = 2


def draw_cache_keys(key, part):
    shape = (N_ROLE, ROWS, CACHE, KVD)
    scaled = jnp.clip(2.0 * jax.random.normal(key, shape, jnp.float32), -12.0, 12.0)
    return scaled.astype(jnp.bfloat16)


def draw_lengths(key, part):
    base = jax.random.randint(key, (N_ROLE, ROWS), 2, CACHE + 1, dtype=jnp.int32)
    groups = ROWS // ROWS_DEV
    chosen = jax.random.randint(jax.random.fold_in(key, 7), (N_ROLE, groups, 1), 0, ROWS_DEV, dtype=jnp.int32)
    within = jnp.arange(ROWS_DEV, dtype=jnp.int32).reshape(1, 1, ROWS_DEV)
    filled = (within == chosen).reshape(N_ROLE, ROWS)
    return jnp.where(filled, CACHE, base).astype(jnp.int32)


def levels(own_key, extent, cuts, low, largest):
    def one(dim, blocks):
        draws = jax.random.uniform(jax.random.fold_in(jax.random.fold_in(own_key, 6), dim), (blocks,), jnp.float32, low / len(cuts), largest / len(cuts))
        return jnp.repeat(jnp.exp(draws), extent[dim] // blocks).reshape((-1,) + (1,) * (len(extent) - dim - 1))

    loudness = one(*cuts[0])
    for cut in cuts[1:]:
        loudness = loudness * one(*cut)
    return loudness


def noise(key, dims, scale, limit, split=(), kind=jnp.bfloat16):
    entries = jax.random.normal(key, dims, jnp.float32) * scale
    if len(split) > 0:
        entries = levels(key, dims, split, -0.22, 0.18) * entries
    return jnp.clip(entries, min=-limit, max=limit).astype(kind)


def setup_inputs(seed: int = 0) -> dict:
    key_of = jax.random.split(jax.random.key(seed), 9)
    return {
        "qkv_versions": noise(key_of[0], (N_ROLE, D, QKV), D ** -0.5, 0.078125, ((0, 2), (1, 4), (2, 16))),
        "qkv_bias": noise(key_of[1], (N_ROLE, QKV), 0.5, 3.0, ((0, 2),)),
        "o_versions": noise(key_of[2], (N_ROLE, QDIM, D), QDIM ** -0.5, 0.078125, ((0, 2), (1, 4), (2, 16))),
        "norm_gain": jnp.clip(1.0 + 0.1 * jax.random.normal(key_of[3], (N_ROLE, D), jnp.float32), 0.5, 1.5).astype(jnp.bfloat16),
        "hidden": noise(key_of[4], (N_ROLE, ROWS, STEPS, D), 1.0, 6.0, ((0, 2), (1, 64))),
        "cache_keys": draw_cache_keys(jax.random.fold_in(key_of[8], 71), 0),
        "cache_values": noise(key_of[6], (N_ROLE, ROWS, CACHE, KVD), 1.0, 6.0, ((0, 2), (1, 64))),
        "lengths": draw_lengths(jax.random.fold_in(key_of[8], 71), 0),
    }


EPSILON = 1e-06
ROPE_BASE = 1000000.0

def hadamard_pair():
    modulus = FACTOR_A // 2 - 1
    residues = jnp.arange(modulus, dtype=jnp.int32)
    squares = jnp.arange(1, modulus, dtype=jnp.int32) ** 2 % modulus
    differ = (residues[None, :] - residues[:, None]) % modulus
    residue_mask = jnp.any(differ[:, :, None] == squares[None, None, :], axis=2)
    jacobs = jnp.where(differ == 0, 0.0, jnp.where(residue_mask, 1.0, -1.0)).astype(jnp.float32)
    top_row = jnp.concatenate([jnp.zeros((1, 1), jnp.float32), jnp.ones((1, modulus), jnp.float32)], axis=1)
    lower_rows = jnp.concatenate([-jnp.ones((modulus, 1), jnp.float32), jacobs], axis=1)
    paley_core = jnp.eye(modulus + 1, dtype=jnp.float32) + jnp.concatenate([top_row, lower_rows], axis=0)
    doubler = jnp.array([[1.0, 1.0], [1.0, -1.0]], jnp.float32)
    outer_factor = jnp.kron(doubler, paley_core)
    indices = jnp.arange(FACTOR_B, dtype=jnp.int32)
    common_bits = indices[:, None] & indices[None, :]
    parity = jnp.zeros((FACTOR_B, FACTOR_B), jnp.int32)
    for bit_level in range(FACTOR_B.bit_length() - 1):
        parity = parity + (common_bits >> bit_level & 1)
    inner_factor = (1 - 2 * (parity % 2)).astype(jnp.float32)
    return (outer_factor, inner_factor)

def rotate_rows(matrix):
    outer_factor, inner_factor = hadamard_pair()
    blocks = matrix.reshape(FACTOR_A, FACTOR_B, -1)
    turned = jnp.einsum('abc,ax,by->xyc', blocks, outer_factor, inner_factor, precision=lax.Precision.HIGHEST)
    return turned.reshape(D, -1) / math.sqrt(D)

def rotary(vectors, positions):
    half_dim = HEAD_DIM // 2
    frequency = jnp.power(jnp.float32(ROPE_BASE), -jnp.arange(0, HEAD_DIM, 2, dtype=jnp.float32) / HEAD_DIM)
    angles = positions.astype(jnp.float32)[:, :, None] * frequency[None, None, :]
    cosine = jnp.cos(angles)[:, :, None, :]
    sine = jnp.sin(angles)[:, :, None, :]
    first, second = (vectors[..., :half_dim], vectors[..., half_dim:])
    return jnp.concatenate([first * cosine - second * sine, second * cosine + first * sine], axis=-1)

def normalize(states, gain):
    mean_square = lax.optimization_barrier(jnp.mean(states * states, axis=-1, keepdims=True))
    return (states * lax.rsqrt(mean_square + EPSILON) * gain.astype(jnp.float32)).astype(jnp.bfloat16)

def attend(packed, keys, values, lengths):
    rows = packed.shape[0]
    group_size = HEADS // KV_HEADS
    positions = lengths[:, None] + jnp.arange(STEPS, dtype=jnp.int32)[None, :]
    queries = rotary(packed[:, :, :QDIM].astype(jnp.float32).reshape(rows, STEPS, HEADS, HEAD_DIM), positions).astype(jnp.bfloat16)
    new_keys = rotary(packed[:, :, QDIM:QDIM + KVD].astype(jnp.float32).reshape(rows, STEPS, KV_HEADS, HEAD_DIM), positions).astype(jnp.bfloat16)
    new_values = packed[:, :, QDIM + KVD:].reshape(rows, STEPS, KV_HEADS, HEAD_DIM)
    queries = queries.reshape(rows, STEPS, KV_HEADS, group_size, HEAD_DIM).astype(jnp.float32)
    cached_keys = keys.reshape(rows, CACHE, KV_HEADS, HEAD_DIM).astype(jnp.float32)
    cached_values = values.reshape(rows, CACHE, KV_HEADS, HEAD_DIM).astype(jnp.float32)
    score_scale = 1.0 / math.sqrt(HEAD_DIM)
    old_scores = jnp.einsum('rtkgd,rpkd->rtkgp', queries, cached_keys) * score_scale
    fresh_scores = jnp.einsum('rtkgd,rskd->rtkgs', queries, new_keys.astype(jnp.float32)) * score_scale
    live_mask = jnp.arange(CACHE, dtype=jnp.int32)[None, :] < lengths[:, None]
    old_scores = jnp.where(live_mask[:, None, None, None, :], old_scores, -1e+30)
    causal = jnp.arange(STEPS, dtype=jnp.int32)[None, :] <= jnp.arange(STEPS, dtype=jnp.int32)[:, None]
    fresh_scores = jnp.where(causal[None, :, None, None, :], fresh_scores, -1e+30)
    row_peak = jnp.maximum(lax.optimization_barrier(jnp.max(old_scores, axis=-1, keepdims=True)), lax.optimization_barrier(jnp.max(fresh_scores, axis=-1, keepdims=True)))
    old_exp = jnp.exp(old_scores - row_peak)
    fresh_exp = jnp.exp(fresh_scores - row_peak)
    denominator = lax.optimization_barrier(jnp.sum(old_exp, axis=-1, keepdims=True)) + lax.optimization_barrier(jnp.sum(fresh_exp, axis=-1, keepdims=True))
    old_weights = (old_exp / denominator).astype(jnp.bfloat16).astype(jnp.float32)
    fresh_weights = (fresh_exp / denominator).astype(jnp.bfloat16).astype(jnp.float32)
    combined = jnp.einsum('rtkgp,rpkd->rtkgd', old_weights, cached_values)
    combined = combined + jnp.einsum('rtkgs,rskd->rtkgd', fresh_weights, new_values.astype(jnp.float32))
    return combined.reshape(rows, STEPS, QDIM).astype(jnp.bfloat16)

def layer_forward(qkv_weight, bias, out_weight, gain, hidden, keys, values, lengths):
    states = hidden.astype(jnp.float32)
    normed = normalize(states, gain)
    flat_rows = normed.reshape(-1, D)
    packed = jnp.dot(flat_rows, qkv_weight, preferred_element_type=jnp.float32) + bias.astype(jnp.float32)
    packed = packed.astype(jnp.bfloat16).reshape(ROWS, STEPS, QKV)
    blocks = ROWS // ROWS_DEV

    def one_block(items):
        return attend(items[0], items[1], items[2], items[3])
    attended = lax.map(one_block, (packed.reshape(blocks, ROWS_DEV, STEPS, QKV), keys.reshape(blocks, ROWS_DEV, CACHE, KVD), values.reshape(blocks, ROWS_DEV, CACHE, KVD), lengths.reshape(blocks, ROWS_DEV)))
    attended = attended.reshape(ROWS * STEPS, QDIM)
    projected = jnp.dot(attended, out_weight, preferred_element_type=jnp.float32).reshape(ROWS, STEPS, D)
    return (states + projected).astype(jnp.bfloat16)

def reference(qkv_versions, qkv_bias, o_versions, norm_gain, hidden, cache_keys, cache_values, lengths):
    outputs = []
    for role_slot in range(N_ROLE):
        outputs.append(layer_forward(qkv_versions[role_slot], qkv_bias[role_slot], o_versions[role_slot], norm_gain[role_slot], hidden[role_slot], cache_keys[role_slot], cache_values[role_slot], lengths[role_slot]))
    layer_out = jnp.stack(outputs)
    rotated_qkv = rotate_rows(qkv_versions[0].astype(jnp.float32)).astype(jnp.bfloat16)
    rotated_o = rotate_rows(o_versions[0].astype(jnp.float32).T).T.astype(jnp.bfloat16)
    new_qkv = jnp.stack([rotated_qkv] * N_ROLE)
    new_o = jnp.stack([rotated_o] * N_ROLE)
    return (layer_out, new_qkv, new_o)
```

```python
import math

import jax
import jax.numpy as jnp
from jax import lax
from jax.sharding import PartitionSpec as P

FACTOR_A = 40
FACTOR_B = 128
D = 5120
HEADS = 40
KV_HEADS = 8
HEAD_DIM = 128
QDIM = 5120
KVD = 1024
STEPS = 4


EPSILON = 1e-06
ROPE_BASE = 1000000.0


LINES = 4


def shifted(value, axis, steps):
    count = lax.axis_size(axis)
    initial, last = (max(0, -steps), min(count, count - steps))
    return lax.ppermute(value, axis, [(source, source + steps) for source in range(initial, last)])


def along_z(value, steps):
    count = lax.axis_size("shard")
    pairs = [(s, (s + steps * LINES) % count) for s in range(count)]
    return lax.ppermute(value, "shard", pairs)


def mirror_y(value):
    count = lax.axis_size("shard")
    return lax.ppermute(value, "shard", [(s, s ^ 3) for s in range(count)])


def next_y(value):
    count = lax.axis_size("shard")
    return lax.ppermute(value, "shard", [(s, s ^ 1) for s in range(count)])


def other_chip(value):
    return lax.ppermute(value, "rep", [(r, r ^ 2) for r in range(4)])


def other_core(value):
    return lax.ppermute(value, "rep", [(r, r ^ 1) for r in range(4)])


def gather_rows(own):
    half = own.shape[0] // 2
    below = along_z(own, 1)
    above = along_z(own, -1)
    mirror = mirror_y(own)
    far = jnp.concatenate([along_z(below[:half], 1), along_z(above[half:], -1)], axis=0)
    mirror_below = along_z(mirror, 1)
    mirror_above = along_z(mirror, -1)
    mirror_far = mirror_y(far)
    return (
        jnp.concatenate([own, below, above, far], axis=0),
        jnp.concatenate([mirror, mirror_below, mirror_above, mirror_far], axis=0),
    )


def gather_weights(own):
    half = own.shape[0] // 2
    across = other_chip(own)
    pair = next_y(own)
    beside = other_core(own)
    pair_beside = other_core(pair)
    across_beside = other_core(across)
    pair_across = jnp.concatenate([other_chip(pair[:half]), next_y(across[half:])], axis=0)
    pair_across_beside = other_core(pair_across)
    return (
        jnp.concatenate([own, beside, across, across_beside], axis=0),
        jnp.concatenate([pair, pair_beside, pair_across, pair_across_beside], axis=0),
    )


def slot_columns(rows, rep_index):
    width = rows.shape[1] // 4
    return jnp.concatenate(
        [lax.dynamic_slice_in_dim(rows, (rep_index ^ j) * width, width, 1) for j in range(4)], axis=1
    )


def to_owners(first, second, shard_index):
    count = lax.axis_size("shard")
    line_z = shard_index // LINES
    high = (shard_index // 2) % 2
    rows = first.shape[0] // 4
    both = jnp.stack([first, second]).reshape(8, rows, first.shape[1])
    relative = jnp.array([0, 2, 3, 1], jnp.int32)
    pieces = []
    for owner in range(8):
        distance = (owner // 2 - line_z) % 4
        slot = relative[distance] + 4 * ((owner % 2) ^ high)
        pieces.append(lax.dynamic_index_in_dim(both, slot, 0, keepdims=True))
    ordered = jnp.concatenate(pieces, axis=0)
    lines = count // LINES
    groups = [
        [z * LINES + y for z in range(lines) for y in (0, 3)],
        [z * LINES + y for z in range(lines) for y in (1, 2)],
    ]
    return lax.all_to_all(
        ordered, "shard", split_axis=0, concat_axis=0, axis_index_groups=groups, tiled=True
    )


def paired_product(rows, weights, low_first):
    mine = jnp.dot(rows, weights[0], preferred_element_type=jnp.float32)
    others = jnp.dot(rows, weights[1], preferred_element_type=jnp.float32)
    return jnp.where(
        low_first,
        jnp.concatenate([mine, others], axis=1),
        jnp.concatenate([others, mine], axis=1),
    )


def hadamard_pair():
    modulus = FACTOR_A // 2 - 1
    residues = jnp.arange(modulus, dtype=jnp.int32)
    squares = jnp.arange(1, modulus, dtype=jnp.int32) ** 2 % modulus
    differ = (residues[None, :] - residues[:, None]) % modulus
    residue_mask = jnp.any(differ[:, :, None] == squares[None, None, :], axis=2)
    jacobs = jnp.where(differ == 0, 0.0, jnp.where(residue_mask, 1.0, -1.0)).astype(jnp.float32)
    top_row = jnp.concatenate(
        [jnp.zeros((1, 1), jnp.float32), jnp.ones((1, modulus), jnp.float32)], axis=1
    )
    lower_rows = jnp.concatenate([-jnp.ones((modulus, 1), jnp.float32), jacobs], axis=1)
    paley_core = jnp.eye(modulus + 1, dtype=jnp.float32) + jnp.concatenate(
        [top_row, lower_rows], axis=0
    )
    doubler = jnp.array([[1.0, 1.0], [1.0, -1.0]], jnp.float32)
    outer_factor = jnp.kron(doubler, paley_core)
    indices = jnp.arange(FACTOR_B, dtype=jnp.int32)
    common_bits = indices[:, None] & indices[None, :]
    parity = jnp.zeros((FACTOR_B, FACTOR_B), jnp.int32)
    for bit_level in range(FACTOR_B.bit_length() - 1):
        parity = parity + (common_bits >> bit_level & 1)
    inner_factor = (1 - 2 * (parity % 2)).astype(jnp.float32)
    return (outer_factor, inner_factor)


def rotate_row_part(full_rows, part_index, part_total):
    outer_factor, inner_factor = hadamard_pair()
    blocks = full_rows.reshape(FACTOR_A, FACTOR_B, full_rows.shape[1])
    inner_mixed = jnp.einsum(
        "abc,by->ayc", blocks, inner_factor.astype(jnp.bfloat16), preferred_element_type=jnp.float32
    )
    part_width = FACTOR_A // part_total
    outer_part = lax.dynamic_slice_in_dim(outer_factor, part_index * part_width, part_width, 1)
    outer_part = jnp.concatenate(
        [
            lax.dynamic_slice_in_dim(outer_part, (part_index ^ j) * part_width, part_width, 0)
            for j in range(part_total)
        ],
        axis=0,
    )
    turned = jnp.einsum("ayc,ax->xyc", inner_mixed, outer_part, precision=lax.Precision.HIGHEST)
    return (
        turned.reshape(part_width * FACTOR_B, full_rows.shape[1]) * (1.0 / math.sqrt(D))
    ).astype(jnp.bfloat16)


def rotate_columns(matrix):
    outer_factor, inner_factor = hadamard_pair()
    height = matrix.shape[0]
    blocks = matrix.reshape(height, FACTOR_A, FACTOR_B)
    inner_mixed = jnp.einsum(
        "mab,by->may", blocks, inner_factor.astype(jnp.bfloat16), preferred_element_type=jnp.float32
    )
    turned = jnp.einsum("may,ax->mxy", inner_mixed, outer_factor, precision=lax.Precision.HIGHEST)
    return (turned.reshape(height, D) * (1.0 / math.sqrt(D))).astype(jnp.bfloat16)


def fold_columns(block):
    spread = lax.all_to_all(block, "shard", split_axis=0, concat_axis=1, tiled=True)
    turned = rotate_columns(spread)
    return lax.all_to_all(turned, "shard", split_axis=1, concat_axis=0, tiled=True)


def rotary(vectors, positions):
    half_dim = HEAD_DIM // 2
    frequency = jnp.power(
        jnp.float32(ROPE_BASE), -jnp.arange(0, HEAD_DIM, 2, dtype=jnp.float32) / HEAD_DIM
    )
    angles = positions.astype(jnp.float32)[:, :, None] * frequency[None, None, :]
    cosine = jnp.cos(angles)[:, :, None, :]
    sine = jnp.sin(angles)[:, :, None, :]
    first, second = (vectors[..., :half_dim], vectors[..., half_dim:])
    return jnp.concatenate(
        [first * cosine - second * sine, second * cosine + first * sine], axis=-1
    )


def normalize(states, gain):
    mean_square = jnp.mean(states * states, axis=-1, keepdims=True)
    return (states * lax.rsqrt(mean_square + EPSILON) * gain.astype(jnp.float32)).astype(
        jnp.bfloat16
    )


def attend(packed, keys, values, lengths):
    rows = packed.shape[0]
    cached = keys.shape[1]
    group_size = HEADS // KV_HEADS
    positions = lengths[:, None] + jnp.arange(STEPS, dtype=jnp.int32)[None, :]
    queries = rotary(
        packed[:, :, :QDIM].astype(jnp.float32).reshape(rows, STEPS, HEADS, HEAD_DIM), positions
    ).astype(jnp.bfloat16)
    new_keys = rotary(
        packed[:, :, QDIM : QDIM + KVD]
        .astype(jnp.float32)
        .reshape(rows, STEPS, KV_HEADS, HEAD_DIM),
        positions,
    ).astype(jnp.bfloat16)
    new_values = packed[:, :, QDIM + KVD :].reshape(rows, STEPS, KV_HEADS, HEAD_DIM)
    queries = queries.reshape(rows, STEPS, KV_HEADS, group_size, HEAD_DIM)
    cached_keys = keys.reshape(rows, cached, KV_HEADS, HEAD_DIM)
    cached_values = values.reshape(rows, cached, KV_HEADS, HEAD_DIM)
    score_scale = 1.0 / math.sqrt(HEAD_DIM)
    old_scores = (
        jnp.einsum("rtkgd,rpkd->rtkgp", queries, cached_keys, preferred_element_type=jnp.float32)
        * score_scale
    )
    fresh_scores = (
        jnp.einsum("rtkgd,rskd->rtkgs", queries, new_keys, preferred_element_type=jnp.float32)
        * score_scale
    )
    live_mask = jnp.arange(cached, dtype=jnp.int32)[None, :] < lengths[:, None]
    old_scores = jnp.where(live_mask[:, None, None, None, :], old_scores, -1e30)
    causal = (
        jnp.arange(STEPS, dtype=jnp.int32)[None, :] <= jnp.arange(STEPS, dtype=jnp.int32)[:, None]
    )
    fresh_scores = jnp.where(causal[None, :, None, None, :], fresh_scores, -1e30)
    row_peak = jnp.maximum(
        jnp.max(old_scores, axis=-1, keepdims=True), jnp.max(fresh_scores, axis=-1, keepdims=True)
    )
    old_exp = jnp.exp(old_scores - row_peak)
    fresh_exp = jnp.exp(fresh_scores - row_peak)
    denominator = jnp.sum(old_exp, axis=-1, keepdims=True) + jnp.sum(
        fresh_exp, axis=-1, keepdims=True
    )
    old_weights = (old_exp / denominator).astype(jnp.bfloat16)
    fresh_weights = (fresh_exp / denominator).astype(jnp.bfloat16)
    combined = jnp.einsum(
        "rtkgp,rpkd->rtkgd", old_weights, cached_values, preferred_element_type=jnp.float32
    )
    combined = combined + jnp.einsum(
        "rtkgs,rskd->rtkgd", fresh_weights, new_values, preferred_element_type=jnp.float32
    )
    return combined.reshape(rows, STEPS, QDIM).astype(jnp.bfloat16)


def body(qkv_versions, qkv_bias, o_versions, norm_gain, hidden, cache_keys, cache_values, lengths):
    trainer_side = lax.axis_index("role") == 0
    shard_index = lax.axis_index("shard")
    rep_index = lax.axis_index("rep")
    rep_total = lax.axis_size("rep")
    low_first = shard_index % 2 == 0
    piece_index = shard_index // 2
    own_qkv = qkv_versions[0]
    own_out = o_versions[0]
    states = hidden[0].astype(jnp.float32)
    rows = states.shape[0]
    tokens = rows * STEPS
    normed = normalize(states, norm_gain[0]).reshape(tokens, D)
    qkv_pair = gather_weights(own_qkv)
    out_pair = gather_weights(own_out)
    width = 2 * own_qkv.shape[1]
    bias = lax.dynamic_slice_in_dim(qkv_bias[0], piece_index * width, width).astype(jnp.float32)
    gathered = gather_rows(slot_columns(normed, rep_index))
    first, second = [
        (paired_product(chunk, qkv_pair, low_first) + bias).astype(jnp.bfloat16)
        for chunk in gathered
    ]
    packed = to_owners(first, second, shard_index)
    packed = packed.transpose(1, 0, 2).reshape(rows, STEPS, 8 * width)
    attended = attend(packed, cache_keys[0], cache_values[0], lengths[0]).reshape(tokens, QDIM)
    gathered = gather_rows(slot_columns(attended, rep_index))
    first, second = [
        paired_product(chunk, out_pair, low_first).astype(jnp.bfloat16) for chunk in gathered
    ]
    projected = to_owners(first, second, shard_index)
    projected = projected.transpose(1, 0, 2).reshape(rows, STEPS, D).astype(jnp.float32)
    layer_out = (states + projected).astype(jnp.bfloat16)[None]
    folded_qkv = rotate_row_part(qkv_pair[0], rep_index, rep_total)
    folded_out = fold_columns(own_out)
    sent_qkv, sent_out = shifted((folded_qkv, folded_out), "role", 1)
    new_qkv = jnp.where(trainer_side, folded_qkv, sent_qkv)
    new_o = jnp.where(trainer_side, folded_out, sent_out)
    return (layer_out, new_qkv[None], new_o[None])


def solution(mesh):
    in_specs = (
        P("role", "rep", "shard"),
        P("role", None),
        P("role", "rep", "shard"),
        P("role", None),
        P("role", ("shard", "rep"), None, None),
        P("role", ("shard", "rep"), None, None),
        P("role", ("shard", "rep"), None, None),
        P("role", ("shard", "rep")),
    )
    out_specs = (
        P("role", ("shard", "rep"), None, None),
        P("role", "rep", "shard"),
        P("role", "rep", "shard"),
    )
    return jax.shard_map(body, mesh=mesh, in_specs=in_specs, out_specs=out_specs, check_vma=False)
```

```python
import math

import jax
import jax.numpy as jnp
from jax import lax
from jax.sharding import PartitionSpec as P

FACTOR_A = 40
FACTOR_B = 128
D = 5120
HEADS = 40
KV_HEADS = 8
HEAD_DIM = 128
QDIM = 5120
KVD = 1024
STEPS = 4


EPSILON = 1e-06
ROPE_BASE = 1000000.0


LINES = 4


def shifted(value, axis, steps):
    count = lax.axis_size(axis)
    initial, last = (max(0, -steps), min(count, count - steps))
    return lax.ppermute(value, axis, [(source, source + steps) for source in range(initial, last)])


def along_z(value, steps):
    count = lax.axis_size("shard")
    pairs = [(s, (s + steps * LINES) % count) for s in range(count)]
    return lax.ppermute(value, "shard", pairs)


def mirror_y(value):
    count = lax.axis_size("shard")
    return lax.ppermute(value, "shard", [(s, s ^ 3) for s in range(count)])


def next_y(value):
    count = lax.axis_size("shard")
    return lax.ppermute(value, "shard", [(s, s ^ 1) for s in range(count)])


def other_chip(value):
    return lax.ppermute(value, "rep", [(r, r ^ 2) for r in range(4)])


def other_core(value):
    return lax.ppermute(value, "rep", [(r, r ^ 1) for r in range(4)])


def crossed(even_value, odd_value, even_pair, odd_pair):
    value = jnp.where(lax.axis_index("rep") % 2 == 0, even_value, odd_value)
    reps = lax.axis_size("rep")
    pairs = []
    for s in range(lax.axis_size("shard")):
        for r in range(reps):
            to_shard, to_rep = (even_pair if r % 2 == 0 else odd_pair)(s, r)
            pairs.append((s * reps + r, to_shard * reps + to_rep))
    return lax.ppermute(value, ("shard", "rep"), pairs)


def gather_rows(own):
    count = lax.axis_size("shard")
    below = along_z(own, 1)
    above = along_z(own, -1)
    mirror = mirror_y(own)
    far = crossed(
        below,
        above,
        lambda s, r: ((s + LINES) % count, r),
        lambda s, r: ((s - LINES) % count, r),
    )
    mirror_below = along_z(mirror, 1)
    mirror_above = along_z(mirror, -1)
    mirror_far = mirror_y(far)
    return ((own, below, above, far), (mirror, mirror_below, mirror_above, mirror_far))


def gather_weights(own):
    across = other_chip(own)
    pair = next_y(own)
    beside = other_core(own)
    pair_beside = other_core(pair)
    across_beside = other_core(across)
    pair_across = crossed(
        pair, across, lambda s, r: (s, r ^ 2), lambda s, r: (s ^ 1, r)
    )
    pair_across_beside = other_core(pair_across)
    return (
        (own, beside, across, across_beside),
        (pair, pair_beside, pair_across, pair_across_beside),
    )


def after(value, *others):
    return lax.optimization_barrier((value,) + others)[0]


def slot_columns(rows, rep_index):
    width = rows.shape[1] // 4
    return jnp.concatenate(
        [lax.dynamic_slice_in_dim(rows, (rep_index ^ j) * width, width, 1) for j in range(4)], axis=1
    )


def to_owners(first, second, shard_index):
    count = lax.axis_size("shard")
    line_z = shard_index // LINES
    high = (shard_index // 2) % 2
    rows = first.shape[0] // 4
    both = jnp.stack([first, second]).reshape(8, rows, first.shape[1])
    relative = jnp.array([0, 2, 3, 1], jnp.int32)
    pieces = []
    for owner in range(8):
        distance = (owner // 2 - line_z) % 4
        slot = relative[distance] + 4 * ((owner % 2) ^ high)
        pieces.append(lax.dynamic_index_in_dim(both, slot, 0, keepdims=True))
    ordered = jnp.concatenate(pieces, axis=0)
    lines = count // LINES
    groups = [
        [z * LINES + y for z in range(lines) for y in (0, 3)],
        [z * LINES + y for z in range(lines) for y in (1, 2)],
    ]
    return lax.all_to_all(
        ordered, "shard", split_axis=0, concat_axis=0, axis_index_groups=groups, tiled=True
    )


def paired_product(rows, weights, low_first):
    mine = jnp.dot(rows, weights[0], preferred_element_type=jnp.float32)
    others = jnp.dot(rows, weights[1], preferred_element_type=jnp.float32)
    return jnp.where(
        low_first,
        jnp.concatenate([mine, others], axis=1),
        jnp.concatenate([others, mine], axis=1),
    )


def hadamard_pair():
    modulus = FACTOR_A // 2 - 1
    residues = jnp.arange(modulus, dtype=jnp.int32)
    squares = jnp.arange(1, modulus, dtype=jnp.int32) ** 2 % modulus
    differ = (residues[None, :] - residues[:, None]) % modulus
    residue_mask = jnp.any(differ[:, :, None] == squares[None, None, :], axis=2)
    jacobs = jnp.where(differ == 0, 0.0, jnp.where(residue_mask, 1.0, -1.0)).astype(jnp.float32)
    top_row = jnp.concatenate(
        [jnp.zeros((1, 1), jnp.float32), jnp.ones((1, modulus), jnp.float32)], axis=1
    )
    lower_rows = jnp.concatenate([-jnp.ones((modulus, 1), jnp.float32), jacobs], axis=1)
    paley_core = jnp.eye(modulus + 1, dtype=jnp.float32) + jnp.concatenate(
        [top_row, lower_rows], axis=0
    )
    doubler = jnp.array([[1.0, 1.0], [1.0, -1.0]], jnp.float32)
    outer_factor = jnp.kron(doubler, paley_core)
    indices = jnp.arange(FACTOR_B, dtype=jnp.int32)
    common_bits = indices[:, None] & indices[None, :]
    parity = jnp.zeros((FACTOR_B, FACTOR_B), jnp.int32)
    for bit_level in range(FACTOR_B.bit_length() - 1):
        parity = parity + (common_bits >> bit_level & 1)
    inner_factor = (1 - 2 * (parity % 2)).astype(jnp.float32)
    return (outer_factor, inner_factor)


def rotate_row_part(full_rows, part_index, part_total):
    outer_factor, inner_factor = hadamard_pair()
    blocks = full_rows.reshape(FACTOR_A, FACTOR_B, full_rows.shape[1])
    inner_mixed = jnp.einsum(
        "abc,by->ayc", blocks, inner_factor.astype(jnp.bfloat16), preferred_element_type=jnp.float32
    )
    part_width = FACTOR_A // part_total
    outer_part = lax.dynamic_slice_in_dim(outer_factor, part_index * part_width, part_width, 1)
    outer_part = jnp.concatenate(
        [
            lax.dynamic_slice_in_dim(outer_part, (part_index ^ j) * part_width, part_width, 0)
            for j in range(part_total)
        ],
        axis=0,
    )
    turned = jnp.einsum("ayc,ax->xyc", inner_mixed, outer_part, precision=lax.Precision.HIGHEST)
    return (
        turned.reshape(part_width * FACTOR_B, full_rows.shape[1]) * (1.0 / math.sqrt(D))
    ).astype(jnp.bfloat16)


def rotate_columns(matrix):
    outer_factor, inner_factor = hadamard_pair()
    height = matrix.shape[0]
    blocks = matrix.reshape(height, FACTOR_A, FACTOR_B)
    inner_mixed = jnp.einsum(
        "mab,by->may", blocks, inner_factor.astype(jnp.bfloat16), preferred_element_type=jnp.float32
    )
    turned = jnp.einsum("may,ax->mxy", inner_mixed, outer_factor, precision=lax.Precision.HIGHEST)
    return (turned.reshape(height, D) * (1.0 / math.sqrt(D))).astype(jnp.bfloat16)


def fold_columns(block):
    spread = lax.all_to_all(block, "shard", split_axis=0, concat_axis=1, tiled=True)
    turned = rotate_columns(spread)
    return lax.all_to_all(turned, "shard", split_axis=1, concat_axis=0, tiled=True)


def rotary(vectors, positions):
    half_dim = HEAD_DIM // 2
    frequency = jnp.power(
        jnp.float32(ROPE_BASE), -jnp.arange(0, HEAD_DIM, 2, dtype=jnp.float32) / HEAD_DIM
    )
    angles = positions.astype(jnp.float32)[:, :, None] * frequency[None, None, :]
    cosine = jnp.cos(angles)[:, :, None, :]
    sine = jnp.sin(angles)[:, :, None, :]
    first, second = (vectors[..., :half_dim], vectors[..., half_dim:])
    return jnp.concatenate(
        [first * cosine - second * sine, second * cosine + first * sine], axis=-1
    )


def normalize(states, gain):
    mean_square = jnp.mean(states * states, axis=-1, keepdims=True)
    return (states * lax.rsqrt(mean_square + EPSILON) * gain.astype(jnp.float32)).astype(
        jnp.bfloat16
    )


def attend(packed, keys, values, lengths):
    rows = packed.shape[0]
    cached = keys.shape[1]
    group_size = HEADS // KV_HEADS
    positions = lengths[:, None] + jnp.arange(STEPS, dtype=jnp.int32)[None, :]
    queries = rotary(
        packed[:, :, :QDIM].astype(jnp.float32).reshape(rows, STEPS, HEADS, HEAD_DIM), positions
    ).astype(jnp.bfloat16)
    new_keys = rotary(
        packed[:, :, QDIM : QDIM + KVD]
        .astype(jnp.float32)
        .reshape(rows, STEPS, KV_HEADS, HEAD_DIM),
        positions,
    ).astype(jnp.bfloat16)
    new_values = packed[:, :, QDIM + KVD :].reshape(rows, STEPS, KV_HEADS, HEAD_DIM)
    queries = queries.reshape(rows, STEPS, KV_HEADS, group_size, HEAD_DIM)
    cached_keys = keys.reshape(rows, cached, KV_HEADS, HEAD_DIM)
    cached_values = values.reshape(rows, cached, KV_HEADS, HEAD_DIM)
    score_scale = 1.0 / math.sqrt(HEAD_DIM)
    old_scores = (
        jnp.einsum("rtkgd,rpkd->rtkgp", queries, cached_keys, preferred_element_type=jnp.float32)
        * score_scale
    )
    fresh_scores = (
        jnp.einsum("rtkgd,rskd->rtkgs", queries, new_keys, preferred_element_type=jnp.float32)
        * score_scale
    )
    live_mask = jnp.arange(cached, dtype=jnp.int32)[None, :] < lengths[:, None]
    old_scores = jnp.where(live_mask[:, None, None, None, :], old_scores, -1e30)
    causal = (
        jnp.arange(STEPS, dtype=jnp.int32)[None, :] <= jnp.arange(STEPS, dtype=jnp.int32)[:, None]
    )
    fresh_scores = jnp.where(causal[None, :, None, None, :], fresh_scores, -1e30)
    row_peak = jnp.maximum(
        jnp.max(old_scores, axis=-1, keepdims=True), jnp.max(fresh_scores, axis=-1, keepdims=True)
    )
    old_exp = jnp.exp(old_scores - row_peak)
    fresh_exp = jnp.exp(fresh_scores - row_peak)
    denominator = jnp.sum(old_exp, axis=-1, keepdims=True) + jnp.sum(
        fresh_exp, axis=-1, keepdims=True
    )
    old_weights = (old_exp / denominator).astype(jnp.bfloat16)
    fresh_weights = (fresh_exp / denominator).astype(jnp.bfloat16)
    combined = jnp.einsum(
        "rtkgp,rpkd->rtkgd", old_weights, cached_values, preferred_element_type=jnp.float32
    )
    combined = combined + jnp.einsum(
        "rtkgs,rskd->rtkgd", fresh_weights, new_values, preferred_element_type=jnp.float32
    )
    return combined.reshape(rows, STEPS, QDIM).astype(jnp.bfloat16)


def body(qkv_versions, qkv_bias, o_versions, norm_gain, hidden, cache_keys, cache_values, lengths):
    trainer_side = lax.axis_index("role") == 0
    shard_index = lax.axis_index("shard")
    rep_index = lax.axis_index("rep")
    rep_total = lax.axis_size("rep")
    low_first = shard_index % 2 == 0
    piece_index = shard_index // 2
    own_qkv = qkv_versions[0]
    own_out = o_versions[0]
    states = hidden[0].astype(jnp.float32)
    rows = states.shape[0]
    tokens = rows * STEPS
    normed = normalize(states, norm_gain[0]).reshape(tokens, D)
    qkv_slots = gather_weights(own_qkv)
    out_slots = gather_weights(after(own_out, qkv_slots[1][2]))
    qkv_pair = [jnp.concatenate(part, axis=0) for part in qkv_slots]
    out_pair = [jnp.concatenate(part, axis=0) for part in out_slots]
    width = 2 * own_qkv.shape[1]
    bias = lax.dynamic_slice_in_dim(qkv_bias[0], piece_index * width, width).astype(jnp.float32)
    gathered = gather_rows(slot_columns(normed, rep_index))
    gathered = [jnp.concatenate(part, axis=0) for part in gathered]
    first, second = [
        (paired_product(chunk, qkv_pair, low_first) + bias).astype(jnp.bfloat16)
        for chunk in gathered
    ]
    first_packed, second_packed = first, second
    packed = to_owners(first, second, shard_index)
    packed = packed.transpose(1, 0, 2).reshape(rows, STEPS, 8 * width)
    attended = attend(packed, cache_keys[0], cache_values[0], lengths[0]).reshape(tokens, QDIM)
    gathered = gather_rows(slot_columns(attended, rep_index))
    gathered = [jnp.concatenate(part, axis=0) for part in gathered]
    first, second = [
        paired_product(chunk, out_pair, low_first).astype(jnp.bfloat16) for chunk in gathered
    ]
    projected = to_owners(first, second, shard_index)
    projected = projected.transpose(1, 0, 2).reshape(rows, STEPS, D).astype(jnp.float32)
    layer_out = (states + projected).astype(jnp.bfloat16)[None]
    folded_qkv = rotate_row_part(after(qkv_pair[0], first_packed, second_packed), rep_index, rep_total)
    folded_out = fold_columns(after(own_out, packed))
    sent_qkv, sent_out = shifted((folded_qkv, folded_out), "role", 1)
    new_qkv = jnp.where(trainer_side, folded_qkv, sent_qkv)
    new_o = jnp.where(trainer_side, folded_out, sent_out)
    return (layer_out, new_qkv[None], new_o[None])


def solution(mesh):
    in_specs = (
        P("role", "rep", "shard"),
        P("role", None),
        P("role", "rep", "shard"),
        P("role", None),
        P("role", ("shard", "rep"), None, None),
        P("role", ("shard", "rep"), None, None),
        P("role", ("shard", "rep"), None, None),
        P("role", ("shard", "rep")),
    )
    out_specs = (
        P("role", ("shard", "rep"), None, None),
        P("role", "rep", "shard"),
        P("role", "rep", "shard"),
    )
    return jax.shard_map(body, mesh=mesh, in_specs=in_specs, out_specs=out_specs, check_vma=False)
```

```python
import functools
import math

import jax
import jax.numpy as jnp
from jax import lax
from jax.experimental import pallas as pl
from jax.experimental.pallas import tpu as pltpu
from jax.sharding import PartitionSpec as P

FACTOR_A = 40
FACTOR_B = 128
D = 5120
HEADS = 40
KV_HEADS = 8
HEAD_DIM = 128
QDIM = 5120
KVD = 1024
STEPS = 4


EPSILON = 1e-06
ROPE_BASE = 1000000.0


LINES = 4


def shifted(value, axis, steps):
    count = lax.axis_size(axis)
    initial, last = (max(0, -steps), min(count, count - steps))
    return lax.ppermute(value, axis, [(source, source + steps) for source in range(initial, last)])


def along_z(value, steps):
    count = lax.axis_size("shard")
    pairs = [(s, (s + steps * LINES) % count) for s in range(count)]
    return lax.ppermute(value, "shard", pairs)


def mirror_y(value):
    count = lax.axis_size("shard")
    return lax.ppermute(value, "shard", [(s, s ^ 3) for s in range(count)])


def next_y(value):
    count = lax.axis_size("shard")
    return lax.ppermute(value, "shard", [(s, s ^ 1) for s in range(count)])


def other_chip(value):
    return lax.ppermute(value, "rep", [(r, r ^ 2) for r in range(4)])


def other_core(value):
    return lax.ppermute(value, "rep", [(r, r ^ 1) for r in range(4)])


def crossed(even_value, odd_value, even_pair, odd_pair):
    value = jnp.where(lax.axis_index("rep") % 2 == 0, even_value, odd_value)
    reps = lax.axis_size("rep")
    pairs = []
    for s in range(lax.axis_size("shard")):
        for r in range(reps):
            to_shard, to_rep = (even_pair if r % 2 == 0 else odd_pair)(s, r)
            pairs.append((s * reps + r, to_shard * reps + to_rep))
    return lax.ppermute(value, ("shard", "rep"), pairs)


def gather_rows(own):
    count = lax.axis_size("shard")
    below = along_z(own, 1)
    above = along_z(own, -1)
    mirror = mirror_y(own)
    far = crossed(
        below,
        above,
        lambda s, r: ((s + LINES) % count, r),
        lambda s, r: ((s - LINES) % count, r),
    )
    mirror_below = along_z(mirror, 1)
    mirror_above = along_z(mirror, -1)
    mirror_far = mirror_y(far)
    return ((own, below, above, far), (mirror, mirror_below, mirror_above, mirror_far))


def gather_weights(own):
    across = other_chip(own)
    pair = next_y(own)
    beside = other_core(own)
    pair_beside = other_core(pair)
    across_beside = other_core(across)
    pair_across = crossed(
        pair, across, lambda s, r: (s, r ^ 2), lambda s, r: (s ^ 1, r)
    )
    pair_across_beside = other_core(pair_across)
    return (
        (own, beside, across, across_beside),
        (pair, pair_beside, pair_across, pair_across_beside),
    )


def after(value, *others):
    return lax.optimization_barrier((value,) + others)[0]


def slot_columns(rows, rep_index):
    width = rows.shape[1] // 4
    return jnp.concatenate(
        [lax.dynamic_slice_in_dim(rows, (rep_index ^ j) * width, width, 1) for j in range(4)], axis=1
    )


def owner_order(shard_index):
    line_z = shard_index // LINES
    high = (shard_index // 2) % 2
    steps = jnp.array([0, -1, 1, 2], jnp.int32)
    owners = jnp.mod(line_z + steps, 4) * 2
    low_first = (1 - shard_index % 2).reshape(1)
    return owners + high, owners + 1 - high, low_first.astype(jnp.int32)


def to_owners(ordered):
    lines = lax.axis_size("shard") // LINES
    groups = [
        [z * LINES + y for z in range(lines) for y in (0, 3)],
        [z * LINES + y for z in range(lines) for y in (1, 2)],
    ]
    return lax.all_to_all(
        ordered, "shard", split_axis=0, concat_axis=0, axis_index_groups=groups, tiled=True
    )


def hadamard_pair():
    modulus = FACTOR_A // 2 - 1
    residues = jnp.arange(modulus, dtype=jnp.int32)
    squares = jnp.arange(1, modulus, dtype=jnp.int32) ** 2 % modulus
    differ = (residues[None, :] - residues[:, None]) % modulus
    residue_mask = jnp.any(differ[:, :, None] == squares[None, None, :], axis=2)
    jacobs = jnp.where(differ == 0, 0.0, jnp.where(residue_mask, 1.0, -1.0)).astype(jnp.float32)
    top_row = jnp.concatenate(
        [jnp.zeros((1, 1), jnp.float32), jnp.ones((1, modulus), jnp.float32)], axis=1
    )
    lower_rows = jnp.concatenate([-jnp.ones((modulus, 1), jnp.float32), jacobs], axis=1)
    paley_core = jnp.eye(modulus + 1, dtype=jnp.float32) + jnp.concatenate(
        [top_row, lower_rows], axis=0
    )
    doubler = jnp.array([[1.0, 1.0], [1.0, -1.0]], jnp.float32)
    outer_factor = jnp.kron(doubler, paley_core)
    indices = jnp.arange(FACTOR_B, dtype=jnp.int32)
    common_bits = indices[:, None] & indices[None, :]
    parity = jnp.zeros((FACTOR_B, FACTOR_B), jnp.int32)
    for bit_level in range(FACTOR_B.bit_length() - 1):
        parity = parity + (common_bits >> bit_level & 1)
    inner_factor = (1 - 2 * (parity % 2)).astype(jnp.float32)
    return (outer_factor, inner_factor)


def rotate_column_part(matrix, part_index, part_total):
    outer_factor, inner_factor = hadamard_pair()
    height = matrix.shape[0]
    blocks = matrix.reshape(height, FACTOR_A, FACTOR_B)
    inner_mixed = jnp.einsum(
        "mab,by->may", blocks, inner_factor.astype(jnp.bfloat16), preferred_element_type=jnp.float32
    )
    part_width = FACTOR_A // part_total
    outer_part = lax.dynamic_slice_in_dim(outer_factor, part_index * part_width, part_width, 1)
    outer_part = jnp.concatenate(
        [
            lax.dynamic_slice_in_dim(outer_part, (part_index ^ j) * part_width, part_width, 0)
            for j in range(part_total)
        ],
        axis=0,
    )
    turned = jnp.einsum("may,ax->mxy", inner_mixed, outer_part, precision=lax.Precision.HIGHEST)
    return (turned.reshape(height, part_width * FACTOR_B) * (1.0 / math.sqrt(D))).astype(jnp.bfloat16)


def rotate_columns(matrix):
    outer_factor, inner_factor = hadamard_pair()
    height = matrix.shape[0]
    blocks = matrix.reshape(height, FACTOR_A, FACTOR_B)
    inner_mixed = jnp.einsum(
        "mab,by->may", blocks, inner_factor.astype(jnp.bfloat16), preferred_element_type=jnp.float32
    )
    turned = jnp.einsum("may,ax->mxy", inner_mixed, outer_factor, precision=lax.Precision.HIGHEST)
    return (turned.reshape(height, D) * (1.0 / math.sqrt(D))).astype(jnp.bfloat16)


def fold_columns(block):
    spread = lax.all_to_all(block, "shard", split_axis=0, concat_axis=1, tiled=True)
    turned = rotate_columns(spread)
    return lax.all_to_all(turned, "shard", split_axis=1, concat_axis=0, tiled=True)


def normalize(states, gain):
    mean_square = jnp.mean(states * states, axis=-1, keepdims=True)
    return (states * lax.rsqrt(mean_square + EPSILON) * gain.astype(jnp.float32)).astype(
        jnp.bfloat16
    )


def spun(vectors, cosine, sine):
    return vectors * cosine + pltpu.roll(vectors, HEAD_DIM // 2, 1) * sine


def attention_kernel(
    part_ref, length_ref, packed_ref, cosine_ref, sine_ref, keys_ref, values_ref, out_ref, spun_ref, sum_ref
):
    block = pl.program_id(0)
    group = part_ref[0] ^ pl.program_id(1)
    cached = keys_ref.shape[1]
    rows = keys_ref.shape[0]
    tokens = rows * STEPS
    piece_heads = packed_ref.shape[2] // HEAD_DIM
    ratio = HEADS // KV_HEADS
    cosine = cosine_ref[...]
    sine = sine_ref[...]

    def head(index):
        offset = pl.multiple_of(lax.rem(index, piece_heads) * HEAD_DIM, HEAD_DIM)
        return packed_ref[index // piece_heads, :, pl.ds(offset, HEAD_DIM)]

    for u in range(2 * ratio):
        turned = spun(head(group * 2 * ratio + u).astype(jnp.float32), cosine, sine)
        spun_ref[:, u * HEAD_DIM : (u + 1) * HEAD_DIM] = turned.astype(jnp.bfloat16).astype(jnp.float32)
    scale = 1.0 / math.sqrt(HEAD_DIM)
    count = 2 * STEPS * ratio
    token_of = lax.broadcasted_iota(jnp.int32, (count, 1), 0) % (2 * STEPS)
    second_row = token_of >= STEPS
    old_column = lax.broadcasted_iota(jnp.int32, (count, 2 * cached), 1)
    new_column = lax.broadcasted_iota(jnp.int32, (count, tokens), 1)
    old_start = jnp.where(second_row, cached, 0)
    new_start = jnp.where(second_row, STEPS, 0)
    contract_last = (((1,), (1,)), ((), ()))
    for half in range(2):
        lanes = slice(half * HEAD_DIM, (half + 1) * HEAD_DIM)
        new_keys = spun(head(HEADS + group * 2 + half).astype(jnp.float32), cosine, sine).astype(jnp.bfloat16)
        new_values = head(HEADS + KV_HEADS + group * 2 + half)
        for pair in range(rows // 2):
            span = slice(2 * STEPS * pair, 2 * STEPS * (pair + 1))
            queries = jnp.concatenate(
                [
                    spun_ref[span, (half * ratio + u) * HEAD_DIM : (half * ratio + u + 1) * HEAD_DIM]
                    for u in range(ratio)
                ],
                axis=0,
            ).astype(jnp.bfloat16)
            old_keys = keys_ref[2 * pair : 2 * pair + 2, :, lanes].reshape(2 * cached, HEAD_DIM)
            old_values = values_ref[2 * pair : 2 * pair + 2, :, lanes].reshape(2 * cached, HEAD_DIM)
            row = block * rows + 2 * pair
            live = jnp.where(second_row, length_ref[row + 1], length_ref[row])
            old_scores = lax.dot_general(queries, old_keys, contract_last, preferred_element_type=jnp.float32) * scale
            new_scores = lax.dot_general(queries, new_keys, contract_last, preferred_element_type=jnp.float32) * scale
            old_scores = jnp.where(
                (old_column >= old_start) & (old_column < old_start + live), old_scores, -1e30
            )
            first = 2 * STEPS * pair
            new_scores = jnp.where(
                (new_column >= first + new_start) & (new_column <= first + token_of), new_scores, -1e30
            )
            peak = jnp.maximum(
                jnp.max(old_scores, axis=1, keepdims=True), jnp.max(new_scores, axis=1, keepdims=True)
            )
            old_exp = jnp.exp(old_scores - peak)
            new_exp = jnp.exp(new_scores - peak)
            share = 1.0 / (jnp.sum(old_exp, axis=1, keepdims=True) + jnp.sum(new_exp, axis=1, keepdims=True))
            total = jnp.dot(
                (old_exp * share).astype(jnp.bfloat16), old_values, preferred_element_type=jnp.float32
            ) + jnp.dot(
                (new_exp * share).astype(jnp.bfloat16), new_values, preferred_element_type=jnp.float32
            )
            for u in range(ratio):
                sum_ref[span, (half * ratio + u) * HEAD_DIM : (half * ratio + u + 1) * HEAD_DIM] = total[
                    2 * STEPS * u : 2 * STEPS * (u + 1)
                ]
    out_ref[...] = sum_ref[...].astype(jnp.bfloat16)


def attend_slots(pieces, keys, values, lengths, rep_index):
    rows, cached = keys.shape[0], keys.shape[1]
    block_rows = 8
    tokens = block_rows * STEPS
    positions = (lengths[:, None] + jnp.arange(STEPS, dtype=jnp.int32)[None, :]).reshape(-1)
    frequency = jnp.power(
        jnp.float32(ROPE_BASE), -jnp.arange(0, HEAD_DIM, 2, dtype=jnp.float32) / HEAD_DIM
    )
    angles = positions.astype(jnp.float32)[:, None] * frequency[None, :]
    cosine, sine = jnp.cos(angles), jnp.sin(angles)
    cosine = jnp.concatenate([cosine, cosine], axis=1)
    sine = jnp.concatenate([-sine, sine], axis=1)
    width = QDIM // 4
    pair_width = KVD // 4
    return pl.pallas_call(
        attention_kernel,
        out_shape=jax.ShapeDtypeStruct((rows * STEPS, QDIM), jnp.bfloat16),
        grid_spec=pltpu.PrefetchScalarGridSpec(
            num_scalar_prefetch=2,
            grid=(rows // block_rows, 4),
            in_specs=[
                pl.BlockSpec((pieces.shape[0], tokens, pieces.shape[2]), lambda i, j, p, n: (0, i, 0)),
                pl.BlockSpec((tokens, HEAD_DIM), lambda i, j, p, n: (i, 0)),
                pl.BlockSpec((tokens, HEAD_DIM), lambda i, j, p, n: (i, 0)),
                pl.BlockSpec((block_rows, cached, pair_width), lambda i, j, p, n: (i, 0, p[0] ^ j)),
                pl.BlockSpec((block_rows, cached, pair_width), lambda i, j, p, n: (i, 0, p[0] ^ j)),
            ],
            out_specs=pl.BlockSpec((tokens, width), lambda i, j, p, n: (i, j)),
            scratch_shapes=[
                pltpu.VMEM((tokens, width), jnp.float32),
                pltpu.VMEM((tokens, width), jnp.float32),
            ],
        ),
        cost_estimate=pl.CostEstimate(flops=2_000_000_000, bytes_accessed=10_000_000, transcendentals=2_000_000),
        name="attend_slots",
    )(rep_index.astype(jnp.int32).reshape(1), lengths, pieces, cosine, sine, keys, values)


def product_kernel(blocks, groups, has_other, has_buffer, order_ref, *refs):
    refs = list(refs)
    row_refs = [refs.pop(0) for _ in range(blocks)]
    weight_refs = [refs.pop(0) for _ in range(4 * groups)]
    bias_ref = refs.pop(0)
    other_ref = refs.pop(0) if has_other else None
    if has_buffer:
        refs.pop(0)
    out_ref, rows_vmem, weights_vmem, total, out_vmem, row_sem, weight_sem, out_sem = refs
    height = row_refs[0].shape[0]
    width, depth = weight_refs[0].shape
    row_copies = [
        pltpu.make_async_copy(ref, rows_vmem.at[pl.ds(m * height, height)], row_sem.at[m])
        for m, ref in enumerate(row_refs)
    ]
    for copy in row_copies:
        copy.start()
    for i, ref in enumerate(weight_refs):
        pltpu.make_async_copy(ref, weights_vmem.at[i], weight_sem.at[i]).start()
    total[...] = jnp.zeros_like(total)
    for copy in row_copies:
        copy.wait()

    @pl.loop(0, 4 * groups)
    def _(i):
        pltpu.make_async_copy(weight_refs[0], weights_vmem.at[i], weight_sem.at[i]).wait()
        columns = pl.ds(pl.multiple_of(lax.rem(i, 4) * depth, depth), depth)
        total[i // 4] += lax.dot_general(
            rows_vmem[:, columns],
            weights_vmem[i],
            (((1,), (1,)), ((), ())),
            preferred_element_type=jnp.float32,
        )

    if groups == 1 and not has_other:
        out_ref[...] = (total[0] + bias_ref[...]).astype(jnp.bfloat16)
        return
    low_first = order_ref[blocks] == 1
    if has_other:
        mine = other_ref[...].astype(jnp.float32)
        others = total[0] + bias_ref[...]
    else:
        mine = total[0]
        others = total[1]

    @pl.when(low_first)
    def _():
        out_vmem[...] = jnp.concatenate([mine, others], axis=1).astype(jnp.bfloat16)

    @pl.when(jnp.logical_not(low_first))
    def _():
        out_vmem[...] = jnp.concatenate([others, mine], axis=1).astype(jnp.bfloat16)

    out_copies = [
        pltpu.make_async_copy(out_vmem.at[pl.ds(m * height, height)], out_ref.at[order_ref[m]], out_sem.at[m])
        for m in range(blocks)
    ]
    for copy in out_copies:
        copy.start()
    for copy in out_copies:
        copy.wait()


def product(row_blocks, weights, bias, order, other=None, buffer=None, partial=False):
    blocks = len(row_blocks)
    groups = len(weights) // 4
    height, full = row_blocks[0].shape
    width, depth = weights[0].shape
    anywhere = pl.BlockSpec(memory_space=pl.ANY)
    inside = pl.BlockSpec(memory_space=pltpu.VMEM)
    operands = list(row_blocks) + list(weights) + [bias]
    specs = [anywhere] * (len(operands) - 1) + [inside]
    if other is not None:
        operands.append(other)
        specs.append(inside)
    aliases = {}
    if buffer is not None:
        operands.append(buffer)
        specs.append(anywhere)
        aliases = {len(operands): 0}
    if partial:
        out_shape = jax.ShapeDtypeStruct((blocks * height, width), jnp.bfloat16)
    else:
        out_shape = jax.ShapeDtypeStruct((8, height, 2 * width), jnp.bfloat16)
    return pl.pallas_call(
        functools.partial(product_kernel, blocks, groups, other is not None, buffer is not None),
        out_shape=out_shape,
        grid_spec=pltpu.PrefetchScalarGridSpec(
            num_scalar_prefetch=1,
            grid=(),
            in_specs=specs,
            out_specs=inside if partial else anywhere,
            scratch_shapes=[
                pltpu.VMEM((blocks * height, full), jnp.bfloat16),
                pltpu.VMEM((4 * groups, width, depth), jnp.bfloat16),
                pltpu.VMEM((groups, blocks * height, width), jnp.float32),
                pltpu.VMEM((blocks * height, 2 * width), jnp.bfloat16),
                pltpu.SemaphoreType.DMA((blocks,)),
                pltpu.SemaphoreType.DMA((4 * groups,)),
                pltpu.SemaphoreType.DMA((blocks,)),
            ],
        ),
        input_output_aliases=aliases,
        cost_estimate=pl.CostEstimate(
            flops=2 * blocks * height * full * width * groups,
            bytes_accessed=2 * full * width * groups + 2 * blocks * height * full,
            transcendentals=0,
        ),
        name="product",
    )(order, *operands)


def body(qkv_versions, qkv_bias, o_versions, norm_gain, hidden, cache_keys, cache_values, lengths):
    trainer_side = lax.axis_index("role") == 0
    shard_index = lax.axis_index("shard")
    rep_index = lax.axis_index("rep")
    rep_total = lax.axis_size("rep")
    own_qkv = qkv_versions[0].T
    own_out = o_versions[0]
    states = hidden[0].astype(jnp.float32)
    rows = states.shape[0]
    tokens = rows * STEPS
    near, far, low_first = owner_order(shard_index)
    normed = normalize(states, norm_gain[0]).reshape(tokens, D)
    qkv_slots = gather_weights(own_qkv)
    width = own_qkv.shape[0]
    bias = qkv_bias[0].astype(jnp.float32).reshape(1, -1)
    own_bias = lax.dynamic_slice_in_dim(bias, shard_index * width, width, 1)
    pair_bias = lax.dynamic_slice_in_dim(bias, (shard_index ^ 1) * width, width, 1)
    same, mirror = gather_rows(slot_columns(normed, rep_index))
    order = jnp.concatenate([near, far, low_first])
    mine = product(same + mirror, qkv_slots[0], own_bias, order, partial=True)
    packed = to_owners(product(same + mirror, qkv_slots[1], pair_bias, order, other=mine))
    out_slots = gather_weights(after(own_out.T, qkv_slots[1][2]))
    attended = attend_slots(packed, cache_keys[0], cache_values[0], lengths[0], rep_index)
    same, mirror = gather_rows(attended)
    weights = out_slots[0] + out_slots[1]
    no_bias = jnp.zeros((1, own_out.shape[1]), jnp.float32)
    part = product(same, weights, no_bias, jnp.concatenate([near, low_first]))
    part = product(mirror, weights, no_bias, jnp.concatenate([far, low_first]), buffer=part)
    projected = to_owners(part)
    projected = projected.transpose(1, 0, 2).reshape(rows, STEPS, D).astype(jnp.float32)
    layer_out = (states + projected).astype(jnp.bfloat16)[None]
    folded_qkv = rotate_column_part(
        after(jnp.concatenate(qkv_slots[0], axis=1), attended), rep_index, rep_total
    )
    folded_out = fold_columns(after(own_out, packed))
    sent_qkv, sent_out = shifted((folded_qkv, folded_out), "role", 1)
    new_qkv = jnp.where(trainer_side, folded_qkv, sent_qkv)
    new_o = jnp.where(trainer_side, folded_out, sent_out)
    return (layer_out, new_qkv.T[None], new_o[None])


def solution(mesh):
    in_specs = (
        P("role", "rep", "shard"),
        P("role", None),
        P("role", "rep", "shard"),
        P("role", None),
        P("role", ("shard", "rep"), None, None),
        P("role", ("shard", "rep"), None, None),
        P("role", ("shard", "rep"), None, None),
        P("role", ("shard", "rep")),
    )
    out_specs = (
        P("role", ("shard", "rep"), None, None),
        P("role", "rep", "shard"),
        P("role", "rep", "shard"),
    )
    return jax.shard_map(body, mesh=mesh, in_specs=in_specs, out_specs=out_specs, check_vma=False)
```

```python
import functools
import math

import jax
import jax.numpy as jnp
from jax import lax
from jax.experimental import pallas as pl
from jax.experimental.pallas import tpu as pltpu
from jax.sharding import PartitionSpec as P


FACTOR_A = 40
FACTOR_B = 128
D = 5120
HEADS = 40
KV_HEADS = 8
HEAD_DIM = 128
QDIM = 5120
KVD = 1024
STEPS = 4


EPSILON = 1e-06
ROPE_BASE = 1000000.0


LINES = 4


def shifted(value, axis, steps):
    count = lax.axis_size(axis)
    initial, last = (max(0, -steps), min(count, count - steps))
    return lax.ppermute(value, axis, [(source, source + steps) for source in range(initial, last)])


def along_z(value, steps):
    count = lax.axis_size("shard")
    pairs = [(s, (s + steps * LINES) % count) for s in range(count)]
    return lax.ppermute(value, "shard", pairs)


def mirror_y(value):
    count = lax.axis_size("shard")
    return lax.ppermute(value, "shard", [(s, s ^ 3) for s in range(count)])


def next_y(value):
    count = lax.axis_size("shard")
    return lax.ppermute(value, "shard", [(s, s ^ 1) for s in range(count)])


def other_chip(value):
    return lax.ppermute(value, "rep", [(r, r ^ 2) for r in range(4)])


def other_core(value):
    return lax.ppermute(value, "rep", [(r, r ^ 1) for r in range(4)])


def crossed(even_value, odd_value, even_pair, odd_pair):
    value = jnp.where(lax.axis_index("rep") % 2 == 0, even_value, odd_value)
    reps = lax.axis_size("rep")
    pairs = []
    for s in range(lax.axis_size("shard")):
        for r in range(reps):
            to_shard, to_rep = (even_pair if r % 2 == 0 else odd_pair)(s, r)
            pairs.append((s * reps + r, to_shard * reps + to_rep))
    return lax.ppermute(value, ("shard", "rep"), pairs)


def gather_rows(own):
    count = lax.axis_size("shard")
    below = along_z(own, 1)
    above = along_z(own, -1)
    mirror = mirror_y(own)
    far = crossed(
        below,
        above,
        lambda s, r: ((s + LINES) % count, r),
        lambda s, r: ((s - LINES) % count, r),
    )
    mirror, _ = lax.optimization_barrier((mirror, far))
    mirror_below = along_z(mirror, 1)
    mirror_above = along_z(mirror, -1)
    mirror_far = mirror_y(far)
    return ((own, below, above, far), (mirror, mirror_below, mirror_above, mirror_far))


def gather_weights(own):
    across = other_chip(own)
    pair = next_y(own)
    beside = other_core(own)
    pair_beside = other_core(pair)
    across_beside = other_core(across)
    pair_across = crossed(
        pair, across, lambda s, r: (s, r ^ 2), lambda s, r: (s ^ 1, r)
    )
    pair_across_beside = other_core(pair_across)
    return (
        (own, beside, across, across_beside),
        (pair, pair_beside, pair_across, pair_across_beside),
    )


def after(value, *others):
    return lax.optimization_barrier((value,) + others)[0]


def slot_columns(rows, rep_index):
    width = rows.shape[1] // 4
    return jnp.concatenate(
        [lax.dynamic_slice_in_dim(rows, (rep_index ^ j) * width, width, 1) for j in range(4)], axis=1
    )


def owner_order(shard_index):
    line_z = shard_index // LINES
    high = (shard_index // 2) % 2
    steps = jnp.array([0, -1, 1, 2], jnp.int32)
    owners = jnp.mod(line_z + steps, 4) * 2
    low_first = (1 - shard_index % 2).reshape(1)
    return owners + high, owners + 1 - high, low_first.astype(jnp.int32)


def to_owners(ordered):
    lines = lax.axis_size("shard") // LINES
    groups = [
        [z * LINES + y for z in range(lines) for y in (0, 3)],
        [z * LINES + y for z in range(lines) for y in (1, 2)],
    ]
    return lax.all_to_all(
        ordered, "shard", split_axis=0, concat_axis=0, axis_index_groups=groups, tiled=True
    )


def hadamard_pair():
    modulus = FACTOR_A // 2 - 1
    residues = jnp.arange(modulus, dtype=jnp.int32)
    squares = jnp.arange(1, modulus, dtype=jnp.int32) ** 2 % modulus
    differ = (residues[None, :] - residues[:, None]) % modulus
    residue_mask = jnp.any(differ[:, :, None] == squares[None, None, :], axis=2)
    jacobs = jnp.where(differ == 0, 0.0, jnp.where(residue_mask, 1.0, -1.0)).astype(jnp.float32)
    top_row = jnp.concatenate(
        [jnp.zeros((1, 1), jnp.float32), jnp.ones((1, modulus), jnp.float32)], axis=1
    )
    lower_rows = jnp.concatenate([-jnp.ones((modulus, 1), jnp.float32), jacobs], axis=1)
    paley_core = jnp.eye(modulus + 1, dtype=jnp.float32) + jnp.concatenate(
        [top_row, lower_rows], axis=0
    )
    doubler = jnp.array([[1.0, 1.0], [1.0, -1.0]], jnp.float32)
    outer_factor = jnp.kron(doubler, paley_core)
    indices = jnp.arange(FACTOR_B, dtype=jnp.int32)
    common_bits = indices[:, None] & indices[None, :]
    parity = jnp.zeros((FACTOR_B, FACTOR_B), jnp.int32)
    for bit_level in range(FACTOR_B.bit_length() - 1):
        parity = parity + (common_bits >> bit_level & 1)
    inner_factor = (1 - 2 * (parity % 2)).astype(jnp.float32)
    return (outer_factor, inner_factor)


def rotate_column_part(matrix, part_index, part_total):
    outer_factor, inner_factor = hadamard_pair()
    height = matrix.shape[0]
    blocks = matrix.reshape(height, FACTOR_A, FACTOR_B)
    inner_mixed = jnp.einsum(
        "mab,by->may", blocks, inner_factor.astype(jnp.bfloat16), preferred_element_type=jnp.float32
    )
    part_width = FACTOR_A // part_total
    outer_part = lax.dynamic_slice_in_dim(outer_factor, part_index * part_width, part_width, 1)
    outer_part = jnp.concatenate(
        [
            lax.dynamic_slice_in_dim(outer_part, (part_index ^ j) * part_width, part_width, 0)
            for j in range(part_total)
        ],
        axis=0,
    )
    turned = jnp.einsum("may,ax->mxy", inner_mixed, outer_part, precision=lax.Precision.HIGHEST)
    return (turned.reshape(height, part_width * FACTOR_B) * (1.0 / math.sqrt(D))).astype(jnp.bfloat16)


def rotate_columns(matrix):
    outer_factor, inner_factor = hadamard_pair()
    height = matrix.shape[0]
    blocks = matrix.reshape(height, FACTOR_A, FACTOR_B)
    inner_mixed = jnp.einsum(
        "mab,by->may", blocks, inner_factor.astype(jnp.bfloat16), preferred_element_type=jnp.float32
    )
    turned = jnp.einsum("may,ax->mxy", inner_mixed, outer_factor, precision=lax.Precision.HIGHEST)
    return (turned.reshape(height, D) * (1.0 / math.sqrt(D))).astype(jnp.bfloat16)


def normalize(states, gain):
    mean_square = jnp.mean(states * states, axis=-1, keepdims=True)
    return (states * lax.rsqrt(mean_square + EPSILON) * gain.astype(jnp.float32)).astype(
        jnp.bfloat16
    )


def spun(vectors, cosine, sine):
    return vectors * cosine + pltpu.roll(vectors, HEAD_DIM // 2, 1) * sine


def attention_kernel(
    part_ref, length_ref, packed_ref, cosine_ref, sine_ref, keys_ref, values_ref, out_ref, spun_ref, sum_ref
):
    block = pl.program_id(0)
    group = part_ref[0] ^ pl.program_id(1)
    cached = keys_ref.shape[1]
    rows = keys_ref.shape[0]
    tokens = rows * STEPS
    piece_heads = packed_ref.shape[2] // HEAD_DIM
    ratio = HEADS // KV_HEADS
    cosine = cosine_ref[...]
    sine = sine_ref[...]

    def head(index):
        offset = pl.multiple_of(lax.rem(index, piece_heads) * HEAD_DIM, HEAD_DIM)
        return packed_ref[index // piece_heads, :, pl.ds(offset, HEAD_DIM)]

    for u in range(2 * ratio):
        turned = spun(head(group * 2 * ratio + u).astype(jnp.float32), cosine, sine)
        spun_ref[:, u * HEAD_DIM : (u + 1) * HEAD_DIM] = turned.astype(jnp.bfloat16).astype(jnp.float32)
    scale = 1.0 / math.sqrt(HEAD_DIM)
    pairs = rows // 2
    group_rows = 2 * STEPS * ratio
    count = pairs * group_rows
    place = lax.broadcasted_iota(jnp.int32, (count, 1), 0)
    token_of = (place // group_rows) * (2 * STEPS) + place % (2 * STEPS)
    row_of = token_of // STEPS
    live = jnp.zeros((count, 1), jnp.int32)
    for row in range(rows):
        live = jnp.where(row_of == row, length_ref[block * rows + row], live)
    old_start = (row_of % 2) * cached
    old_column = lax.broadcasted_iota(jnp.int32, (count, 2 * cached), 1) - old_start
    old_kept = (old_column >= 0) & (old_column < live)
    new_column = lax.broadcasted_iota(jnp.int32, (count, tokens), 1)
    new_kept = (new_column >= row_of * STEPS) & (new_column <= token_of)
    contract_last = (((1,), (1,)), ((), ()))

    def columns(half, u):
        return slice((half * ratio + u) * HEAD_DIM, (half * ratio + u + 1) * HEAD_DIM)

    for half in range(2):
        lanes = slice(half * HEAD_DIM, (half + 1) * HEAD_DIM)
        new_keys = spun(head(HEADS + group * 2 + half).astype(jnp.float32), cosine, sine).astype(jnp.bfloat16)
        new_values = head(HEADS + KV_HEADS + group * 2 + half)
        queries = [
            jnp.concatenate(
                [spun_ref[2 * STEPS * pair : 2 * STEPS * (pair + 1), columns(half, u)] for u in range(ratio)],
                axis=0,
            )
            for pair in range(pairs)
        ]
        old_scores = jnp.concatenate(
            [
                lax.dot_general(
                    queries[pair].astype(jnp.bfloat16),
                    keys_ref[2 * pair : 2 * pair + 2, :, lanes].reshape(2 * cached, HEAD_DIM),
                    contract_last,
                    preferred_element_type=jnp.float32,
                )
                for pair in range(pairs)
            ],
            axis=0,
        )
        new_scores = lax.dot_general(
            jnp.concatenate(queries, axis=0).astype(jnp.bfloat16),
            new_keys,
            contract_last,
            preferred_element_type=jnp.float32,
        )
        old_scores = jnp.where(old_kept, old_scores * scale, -1e30)
        new_scores = jnp.where(new_kept, new_scores * scale, -1e30)
        peak = jnp.maximum(
            jnp.max(old_scores, axis=1, keepdims=True), jnp.max(new_scores, axis=1, keepdims=True)
        )
        old_exp = jnp.exp(old_scores - peak)
        new_exp = jnp.exp(new_scores - peak)
        share = 1.0 / (jnp.sum(old_exp, axis=1, keepdims=True) + jnp.sum(new_exp, axis=1, keepdims=True))
        old_weights = old_exp * share
        fresh = jnp.dot(
            (new_exp * share).astype(jnp.bfloat16), new_values, preferred_element_type=jnp.float32
        )
        for pair in range(pairs):
            part = slice(pair * group_rows, (pair + 1) * group_rows)
            total = fresh[part] + jnp.dot(
                old_weights[part].astype(jnp.bfloat16),
                values_ref[2 * pair : 2 * pair + 2, :, lanes].reshape(2 * cached, HEAD_DIM),
                preferred_element_type=jnp.float32,
            )
            for u in range(ratio):
                sum_ref[2 * STEPS * pair : 2 * STEPS * (pair + 1), columns(half, u)] = total[
                    2 * STEPS * u : 2 * STEPS * (u + 1)
                ]
    out_ref[...] = sum_ref[...].astype(jnp.bfloat16)


def attend_slots(pieces, keys, values, lengths, rep_index):
    rows, cached = keys.shape[0], keys.shape[1]
    block_rows = 8
    tokens = block_rows * STEPS
    positions = (lengths[:, None] + jnp.arange(STEPS, dtype=jnp.int32)[None, :]).reshape(-1)
    frequency = jnp.power(
        jnp.float32(ROPE_BASE), -jnp.arange(0, HEAD_DIM, 2, dtype=jnp.float32) / HEAD_DIM
    )
    angles = positions.astype(jnp.float32)[:, None] * frequency[None, :]
    cosine, sine = jnp.cos(angles), jnp.sin(angles)
    cosine = jnp.concatenate([cosine, cosine], axis=1)
    sine = jnp.concatenate([-sine, sine], axis=1)
    width = QDIM // 4
    pair_width = KVD // 4
    return pl.pallas_call(
        attention_kernel,
        out_shape=jax.ShapeDtypeStruct((rows * STEPS, QDIM), jnp.bfloat16),
        grid_spec=pltpu.PrefetchScalarGridSpec(
            num_scalar_prefetch=2,
            grid=(rows // block_rows, 4),
            in_specs=[
                pl.BlockSpec((pieces.shape[0], tokens, pieces.shape[2]), lambda i, j, p, n: (0, i, 0)),
                pl.BlockSpec((tokens, HEAD_DIM), lambda i, j, p, n: (i, 0)),
                pl.BlockSpec((tokens, HEAD_DIM), lambda i, j, p, n: (i, 0)),
                pl.BlockSpec((block_rows, cached, pair_width), lambda i, j, p, n: (i, 0, p[0] ^ j)),
                pl.BlockSpec((block_rows, cached, pair_width), lambda i, j, p, n: (i, 0, p[0] ^ j)),
            ],
            out_specs=pl.BlockSpec((tokens, width), lambda i, j, p, n: (i, j)),
            scratch_shapes=[
                pltpu.VMEM((tokens, width), jnp.float32),
                pltpu.VMEM((tokens, width), jnp.float32),
            ],
        ),
        cost_estimate=pl.CostEstimate(flops=2_000_000_000, bytes_accessed=10_000_000, transcendentals=2_000_000),
        name="attend_slots",
    )(rep_index.astype(jnp.int32).reshape(1), lengths, pieces, cosine, sine, keys, values)


def product_kernel(blocks, groups, has_other, has_buffer, order_ref, *refs):
    refs = list(refs)
    row_refs = [refs.pop(0) for _ in range(blocks)]
    weight_refs = [refs.pop(0) for _ in range(4 * groups)]
    bias_ref = refs.pop(0)
    other_ref = refs.pop(0) if has_other else None
    if has_buffer:
        refs.pop(0)
    out_ref, rows_vmem, weights_vmem, total, out_vmem, row_sem, weight_sem, out_sem = refs
    height = row_refs[0].shape[0]
    _, depth = weight_refs[0].shape

    def row_copy(m, j):
        columns = pl.ds(j * depth, depth) if isinstance(j, int) else pl.ds(pl.multiple_of(j * depth, depth), depth)
        return pltpu.make_async_copy(
            row_refs[m].at[:, columns],
            rows_vmem.at[pl.ds(m * height, height), columns],
            row_sem.at[m, j],
        )

    def weight_copy(i):
        return pltpu.make_async_copy(weight_refs[i], weights_vmem.at[i], weight_sem.at[i])

    for j in range(4):
        weight_copy(j).start()
        for m in range(blocks):
            row_copy(m, j).start()
    for i in range(4, 4 * groups):
        weight_copy(i).start()
    total[...] = jnp.zeros_like(total)

    @pl.loop(0, 4 * groups)
    def _(i):
        pltpu.make_async_copy(weight_refs[0], weights_vmem.at[i], weight_sem.at[i]).wait()

        @pl.when(i < 4)
        def _():
            for m in range(blocks):
                row_copy(m, i).wait()

        columns = pl.ds(pl.multiple_of(lax.rem(i, 4) * depth, depth), depth)
        total[i // 4] += lax.dot_general(
            rows_vmem[:, columns],
            weights_vmem[i],
            (((1,), (1,)), ((), ())),
            preferred_element_type=jnp.float32,
        )

    if groups == 1 and not has_other:
        out_ref[...] = (total[0] + bias_ref[...]).astype(jnp.bfloat16)
        return
    low_first = order_ref[blocks] == 1
    if has_other:
        mine = other_ref[...].astype(jnp.float32)
        others = total[0] + bias_ref[...]
    else:
        mine = total[0]
        others = total[1]

    @pl.when(low_first)
    def _():
        out_vmem[...] = jnp.concatenate([mine, others], axis=1).astype(jnp.bfloat16)

    @pl.when(jnp.logical_not(low_first))
    def _():
        out_vmem[...] = jnp.concatenate([others, mine], axis=1).astype(jnp.bfloat16)

    out_copies = [
        pltpu.make_async_copy(out_vmem.at[pl.ds(m * height, height)], out_ref.at[order_ref[m]], out_sem.at[m])
        for m in range(blocks)
    ]
    for copy in out_copies:
        copy.start()
    for copy in out_copies:
        copy.wait()


def product(row_blocks, weights, bias, order, other=None, buffer=None, partial=False):
    blocks = len(row_blocks)
    groups = len(weights) // 4
    height, full = row_blocks[0].shape
    width, depth = weights[0].shape
    anywhere = pl.BlockSpec(memory_space=pl.ANY)
    inside = pl.BlockSpec(memory_space=pltpu.VMEM)
    operands = list(row_blocks) + list(weights) + [bias]
    specs = [anywhere] * (len(operands) - 1) + [inside]
    if other is not None:
        operands.append(other)
        specs.append(inside)
    aliases = {}
    if buffer is not None:
        operands.append(buffer)
        specs.append(anywhere)
        aliases = {len(operands): 0}
    if partial:
        out_shape = jax.ShapeDtypeStruct((blocks * height, width), jnp.bfloat16)
    else:
        out_shape = jax.ShapeDtypeStruct((8, height, 2 * width), jnp.bfloat16)
    return pl.pallas_call(
        functools.partial(product_kernel, blocks, groups, other is not None, buffer is not None),
        out_shape=out_shape,
        grid_spec=pltpu.PrefetchScalarGridSpec(
            num_scalar_prefetch=1,
            grid=(),
            in_specs=specs,
            out_specs=inside if partial else anywhere,
            scratch_shapes=[
                pltpu.VMEM((blocks * height, full), jnp.bfloat16),
                pltpu.VMEM((4 * groups, width, depth), jnp.bfloat16),
                pltpu.VMEM((groups, blocks * height, width), jnp.float32),
                pltpu.VMEM((blocks * height, 2 * width), jnp.bfloat16),
                pltpu.SemaphoreType.DMA((blocks, 4)),
                pltpu.SemaphoreType.DMA((4 * groups,)),
                pltpu.SemaphoreType.DMA((blocks,)),
            ],
        ),
        input_output_aliases=aliases,
        cost_estimate=pl.CostEstimate(
            flops=2 * blocks * height * full * width * groups,
            bytes_accessed=2 * full * width * groups + 2 * blocks * height * full,
            transcendentals=0,
        ),
        name="product",
    )(order, *operands)


def body(qkv_versions, qkv_bias, o_versions, norm_gain, hidden, cache_keys, cache_values, lengths):
    trainer_side = lax.axis_index("role") == 0
    shard_index = lax.axis_index("shard")
    rep_index = lax.axis_index("rep")
    rep_total = lax.axis_size("rep")
    own_qkv = qkv_versions[0].T
    own_out = o_versions[0]
    states = hidden[0].astype(jnp.float32)
    rows = states.shape[0]
    tokens = rows * STEPS
    near, far, low_first = owner_order(shard_index)
    normed = normalize(states, norm_gain[0]).reshape(tokens, D)
    qkv_slots = gather_weights(own_qkv)
    width = own_qkv.shape[0]
    bias = qkv_bias[0].astype(jnp.float32).reshape(1, -1)
    own_bias = lax.dynamic_slice_in_dim(bias, shard_index * width, width, 1)
    pair_bias = lax.dynamic_slice_in_dim(bias, (shard_index ^ 1) * width, width, 1)
    same, mirror = gather_rows(slot_columns(normed, rep_index))
    order = jnp.concatenate([near, far, low_first])
    folded_qkv = rotate_column_part(
        after(jnp.concatenate(qkv_slots[0], axis=1), same[3]), rep_index, rep_total
    )
    mine = product(same + mirror, qkv_slots[0], own_bias, after(order, folded_qkv), partial=True)
    part = product(same + mirror, qkv_slots[1], pair_bias, order, other=mine)
    packed = to_owners(part)
    spread = lax.all_to_all(
        after(own_out, part), "shard", split_axis=0, concat_axis=1, tiled=True
    )
    out_slots = gather_weights(after(own_out.T, qkv_slots[1][2]))
    attended = attend_slots(packed, cache_keys[0], cache_values[0], lengths[0], rep_index)
    same, mirror = gather_rows(attended)
    weights = out_slots[0] + out_slots[1]
    no_bias = jnp.zeros((1, own_out.shape[1]), jnp.float32)
    part = product(same, weights, no_bias, jnp.concatenate([near, low_first]))
    turned = after(rotate_columns(after(spread, attended)), part)
    folded_out = lax.all_to_all(turned, "shard", split_axis=1, concat_axis=0, tiled=True)
    part = product(mirror, weights, no_bias, jnp.concatenate([far, low_first]), buffer=part)
    projected = to_owners(part)
    projected = projected.transpose(1, 0, 2).reshape(rows, STEPS, D).astype(jnp.float32)
    layer_out = (states + projected).astype(jnp.bfloat16)[None]
    sent_qkv, sent_out = shifted((folded_qkv, folded_out), "role", 1)
    new_qkv = jnp.where(trainer_side, folded_qkv, sent_qkv)
    new_o = jnp.where(trainer_side, folded_out, sent_out)
    return (layer_out, new_qkv.T[None], new_o[None])


def solution(mesh):
    in_specs = (
        P("role", "rep", "shard"),
        P("role", None),
        P("role", "rep", "shard"),
        P("role", None),
        P("role", ("shard", "rep"), None, None),
        P("role", ("shard", "rep"), None, None),
        P("role", ("shard", "rep"), None, None),
        P("role", ("shard", "rep")),
    )
    out_specs = (
        P("role", ("shard", "rep"), None, None),
        P("role", "rep", "shard"),
        P("role", "rep", "shard"),
    )
    return jax.shard_map(body, mesh=mesh, in_specs=in_specs, out_specs=out_specs, check_vma=False)
```

```python
import functools
import math

import jax
import jax.numpy as jnp
from jax import lax
from jax.experimental import pallas as pl
from jax.experimental.pallas import tpu as pltpu
from jax.sharding import PartitionSpec as P


FACTOR_A = 40
FACTOR_B = 128
D = 5120
HEADS = 40
KV_HEADS = 8
HEAD_DIM = 128
QDIM = 5120
KVD = 1024
STEPS = 4


EPSILON = 1e-06
ROPE_BASE = 1000000.0


LINES = 4


def shifted(value, axis, steps):
    count = lax.axis_size(axis)
    initial, last = (max(0, -steps), min(count, count - steps))
    return lax.ppermute(value, axis, [(source, source + steps) for source in range(initial, last)])


def along_z(value, steps):
    count = lax.axis_size("shard")
    pairs = [(s, (s + steps * LINES) % count) for s in range(count)]
    return lax.ppermute(value, "shard", pairs)


def mirror_y(value):
    count = lax.axis_size("shard")
    return lax.ppermute(value, "shard", [(s, s ^ 3) for s in range(count)])


def next_y(value):
    count = lax.axis_size("shard")
    return lax.ppermute(value, "shard", [(s, s ^ 1) for s in range(count)])


def other_chip(value):
    return lax.ppermute(value, "rep", [(r, r ^ 2) for r in range(4)])


def other_core(value):
    return lax.ppermute(value, "rep", [(r, r ^ 1) for r in range(4)])


def crossed(even_value, odd_value, even_pair, odd_pair):
    value = jnp.where(lax.axis_index("rep") % 2 == 0, even_value, odd_value)
    reps = lax.axis_size("rep")
    pairs = []
    for s in range(lax.axis_size("shard")):
        for r in range(reps):
            to_shard, to_rep = (even_pair if r % 2 == 0 else odd_pair)(s, r)
            pairs.append((s * reps + r, to_shard * reps + to_rep))
    return lax.ppermute(value, ("shard", "rep"), pairs)


def gather_rows(own):
    count = lax.axis_size("shard")
    below = along_z(own, 1)
    above = along_z(own, -1)
    mirror = mirror_y(own)
    far = crossed(
        below,
        above,
        lambda s, r: ((s + LINES) % count, r),
        lambda s, r: ((s - LINES) % count, r),
    )
    mirror, _ = lax.optimization_barrier((mirror, far))
    mirror_below = along_z(mirror, 1)
    mirror_above = along_z(mirror, -1)
    mirror_far = mirror_y(far)
    return ((own, below, above, far), (mirror, mirror_below, mirror_above, mirror_far))


def gather_weights(own):
    across = other_chip(own)
    pair = next_y(own)
    beside = other_core(own)
    pair_beside = other_core(pair)
    across_beside = other_core(across)
    pair_across = crossed(
        pair, across, lambda s, r: (s, r ^ 2), lambda s, r: (s ^ 1, r)
    )
    pair_across_beside = other_core(pair_across)
    return (
        (own, beside, across, across_beside),
        (pair, pair_beside, pair_across, pair_across_beside),
    )


def after(value, *others):
    return lax.optimization_barrier((value,) + others)[0]


def slot_columns(rows, rep_index):
    width = rows.shape[1] // 4
    return jnp.concatenate(
        [lax.dynamic_slice_in_dim(rows, (rep_index ^ j) * width, width, 1) for j in range(4)], axis=1
    )


def owner_order(shard_index):
    line_z = shard_index // LINES
    high = (shard_index // 2) % 2
    steps = jnp.array([0, -1, 1, 2], jnp.int32)
    owners = jnp.mod(line_z + steps, 4) * 2
    low_first = (1 - shard_index % 2).reshape(1)
    return owners + high, owners + 1 - high, low_first.astype(jnp.int32)


def to_owners(ordered):
    lines = lax.axis_size("shard") // LINES
    groups = [
        [z * LINES + y for z in range(lines) for y in (0, 3)],
        [z * LINES + y for z in range(lines) for y in (1, 2)],
    ]
    return lax.all_to_all(
        ordered, "shard", split_axis=0, concat_axis=0, axis_index_groups=groups, tiled=True
    )


def hadamard_pair():
    modulus = FACTOR_A // 2 - 1
    residues = jnp.arange(modulus, dtype=jnp.int32)
    squares = jnp.arange(1, modulus, dtype=jnp.int32) ** 2 % modulus
    differ = (residues[None, :] - residues[:, None]) % modulus
    residue_mask = jnp.any(differ[:, :, None] == squares[None, None, :], axis=2)
    jacobs = jnp.where(differ == 0, 0.0, jnp.where(residue_mask, 1.0, -1.0)).astype(jnp.float32)
    top_row = jnp.concatenate(
        [jnp.zeros((1, 1), jnp.float32), jnp.ones((1, modulus), jnp.float32)], axis=1
    )
    lower_rows = jnp.concatenate([-jnp.ones((modulus, 1), jnp.float32), jacobs], axis=1)
    paley_core = jnp.eye(modulus + 1, dtype=jnp.float32) + jnp.concatenate(
        [top_row, lower_rows], axis=0
    )
    doubler = jnp.array([[1.0, 1.0], [1.0, -1.0]], jnp.float32)
    outer_factor = jnp.kron(doubler, paley_core)
    indices = jnp.arange(FACTOR_B, dtype=jnp.int32)
    common_bits = indices[:, None] & indices[None, :]
    parity = jnp.zeros((FACTOR_B, FACTOR_B), jnp.int32)
    for bit_level in range(FACTOR_B.bit_length() - 1):
        parity = parity + (common_bits >> bit_level & 1)
    inner_factor = (1 - 2 * (parity % 2)).astype(jnp.float32)
    return (outer_factor, inner_factor)


def rotate_column_part(matrix, part_index, part_total):
    outer_factor, inner_factor = hadamard_pair()
    height = matrix.shape[0]
    blocks = matrix.reshape(height, FACTOR_A, FACTOR_B)
    inner_mixed = jnp.einsum(
        "mab,by->may", blocks, inner_factor.astype(jnp.bfloat16), preferred_element_type=jnp.float32
    )
    part_width = FACTOR_A // part_total
    outer_part = lax.dynamic_slice_in_dim(outer_factor, part_index * part_width, part_width, 1)
    outer_part = jnp.concatenate(
        [
            lax.dynamic_slice_in_dim(outer_part, (part_index ^ j) * part_width, part_width, 0)
            for j in range(part_total)
        ],
        axis=0,
    )
    turned = jnp.einsum("may,ax->mxy", inner_mixed, outer_part, precision=lax.Precision.HIGHEST)
    return (turned.reshape(height, part_width * FACTOR_B) * (1.0 / math.sqrt(D))).astype(jnp.bfloat16)


def rotate_columns(matrix):
    outer_factor, inner_factor = hadamard_pair()
    height = matrix.shape[0]
    blocks = matrix.reshape(height, FACTOR_A, FACTOR_B)
    inner_mixed = jnp.einsum(
        "mab,by->may", blocks, inner_factor.astype(jnp.bfloat16), preferred_element_type=jnp.float32
    )
    turned = jnp.einsum("may,ax->mxy", inner_mixed, outer_factor, precision=lax.Precision.HIGHEST)
    return (turned.reshape(height, D) * (1.0 / math.sqrt(D))).astype(jnp.bfloat16)


def normalize(states, gain):
    mean_square = jnp.mean(states * states, axis=-1, keepdims=True)
    return (states * lax.rsqrt(mean_square + EPSILON) * gain.astype(jnp.float32)).astype(
        jnp.bfloat16
    )


def spun(vectors, cosine, sine):
    return vectors * cosine + pltpu.roll(vectors, HEAD_DIM // 2, 1) * sine


def attention_kernel(
    part_ref, length_ref, packed_ref, cosine_ref, sine_ref, keys_ref, values_ref, out_ref, spun_ref, sum_ref
):
    block = pl.program_id(0)
    group = part_ref[0] ^ pl.program_id(1)
    cached = keys_ref.shape[1]
    rows = keys_ref.shape[0]
    tokens = rows * STEPS
    piece_heads = packed_ref.shape[2] // HEAD_DIM
    ratio = HEADS // KV_HEADS
    cosine = cosine_ref[...]
    sine = sine_ref[...]

    def head(index):
        offset = pl.multiple_of(lax.rem(index, piece_heads) * HEAD_DIM, HEAD_DIM)
        return packed_ref[index // piece_heads, :, pl.ds(offset, HEAD_DIM)]

    for u in range(2 * ratio):
        turned = spun(head(group * 2 * ratio + u).astype(jnp.float32), cosine, sine)
        spun_ref[:, u * HEAD_DIM : (u + 1) * HEAD_DIM] = turned.astype(jnp.bfloat16).astype(jnp.float32)
    scale = 1.0 / math.sqrt(HEAD_DIM)
    pairs = rows // 2
    group_rows = 2 * STEPS * ratio
    count = pairs * group_rows
    place = lax.broadcasted_iota(jnp.int32, (count, 1), 0)
    token_of = (place // group_rows) * (2 * STEPS) + place % (2 * STEPS)
    row_of = token_of // STEPS
    live = jnp.zeros((count, 1), jnp.int32)
    for row in range(rows):
        live = jnp.where(row_of == row, length_ref[block * rows + row], live)
    old_start = (row_of % 2) * cached
    old_column = lax.broadcasted_iota(jnp.int32, (count, 2 * cached), 1) - old_start
    old_kept = (old_column >= 0) & (old_column < live)
    new_column = lax.broadcasted_iota(jnp.int32, (count, tokens), 1)
    new_kept = (new_column >= row_of * STEPS) & (new_column <= token_of)
    contract_last = (((1,), (1,)), ((), ()))

    def columns(half, u):
        return slice((half * ratio + u) * HEAD_DIM, (half * ratio + u + 1) * HEAD_DIM)

    for half in range(2):
        lanes = slice(half * HEAD_DIM, (half + 1) * HEAD_DIM)
        new_keys = spun(head(HEADS + group * 2 + half).astype(jnp.float32), cosine, sine).astype(jnp.bfloat16)
        new_values = head(HEADS + KV_HEADS + group * 2 + half)
        queries = [
            jnp.concatenate(
                [spun_ref[2 * STEPS * pair : 2 * STEPS * (pair + 1), columns(half, u)] for u in range(ratio)],
                axis=0,
            )
            for pair in range(pairs)
        ]
        old_scores = jnp.concatenate(
            [
                lax.dot_general(
                    queries[pair].astype(jnp.bfloat16),
                    keys_ref[2 * pair : 2 * pair + 2, :, lanes].reshape(2 * cached, HEAD_DIM),
                    contract_last,
                    preferred_element_type=jnp.float32,
                )
                for pair in range(pairs)
            ],
            axis=0,
        )
        new_scores = lax.dot_general(
            jnp.concatenate(queries, axis=0).astype(jnp.bfloat16),
            new_keys,
            contract_last,
            preferred_element_type=jnp.float32,
        )
        old_scores = jnp.where(old_kept, old_scores * scale, -1e30)
        new_scores = jnp.where(new_kept, new_scores * scale, -1e30)
        peak = jnp.maximum(
            jnp.max(old_scores, axis=1, keepdims=True), jnp.max(new_scores, axis=1, keepdims=True)
        )
        old_exp = jnp.exp(old_scores - peak)
        new_exp = jnp.exp(new_scores - peak)
        share = 1.0 / (jnp.sum(old_exp, axis=1, keepdims=True) + jnp.sum(new_exp, axis=1, keepdims=True))
        old_weights = old_exp * share
        fresh = jnp.dot(
            (new_exp * share).astype(jnp.bfloat16), new_values, preferred_element_type=jnp.float32
        )
        for pair in range(pairs):
            part = slice(pair * group_rows, (pair + 1) * group_rows)
            total = fresh[part] + jnp.dot(
                old_weights[part].astype(jnp.bfloat16),
                values_ref[2 * pair : 2 * pair + 2, :, lanes].reshape(2 * cached, HEAD_DIM),
                preferred_element_type=jnp.float32,
            )
            for u in range(ratio):
                sum_ref[2 * STEPS * pair : 2 * STEPS * (pair + 1), columns(half, u)] = total[
                    2 * STEPS * u : 2 * STEPS * (u + 1)
                ]
    out_ref[...] = sum_ref[...].astype(jnp.bfloat16)


def attend_slots(pieces, keys, values, lengths, rep_index):
    rows, cached = keys.shape[0], keys.shape[1]
    block_rows = 8
    tokens = block_rows * STEPS
    positions = (lengths[:, None] + jnp.arange(STEPS, dtype=jnp.int32)[None, :]).reshape(-1)
    frequency = jnp.power(
        jnp.float32(ROPE_BASE), -jnp.arange(0, HEAD_DIM, 2, dtype=jnp.float32) / HEAD_DIM
    )
    angles = positions.astype(jnp.float32)[:, None] * frequency[None, :]
    cosine, sine = jnp.cos(angles), jnp.sin(angles)
    cosine = jnp.concatenate([cosine, cosine], axis=1)
    sine = jnp.concatenate([-sine, sine], axis=1)
    width = QDIM // 4
    pair_width = KVD // 4
    return pl.pallas_call(
        attention_kernel,
        out_shape=jax.ShapeDtypeStruct((rows * STEPS, QDIM), jnp.bfloat16),
        grid_spec=pltpu.PrefetchScalarGridSpec(
            num_scalar_prefetch=2,
            grid=(rows // block_rows, 4),
            in_specs=[
                pl.BlockSpec((pieces.shape[0], tokens, pieces.shape[2]), lambda i, j, p, n: (0, i, 0)),
                pl.BlockSpec((tokens, HEAD_DIM), lambda i, j, p, n: (i, 0)),
                pl.BlockSpec((tokens, HEAD_DIM), lambda i, j, p, n: (i, 0)),
                pl.BlockSpec((block_rows, cached, pair_width), lambda i, j, p, n: (i, 0, p[0] ^ j)),
                pl.BlockSpec((block_rows, cached, pair_width), lambda i, j, p, n: (i, 0, p[0] ^ j)),
            ],
            out_specs=pl.BlockSpec((tokens, width), lambda i, j, p, n: (i, j)),
            scratch_shapes=[
                pltpu.VMEM((tokens, width), jnp.float32),
                pltpu.VMEM((tokens, width), jnp.float32),
            ],
        ),
        cost_estimate=pl.CostEstimate(flops=2_000_000_000, bytes_accessed=10_000_000, transcendentals=2_000_000),
        name="attend_slots",
    )(rep_index.astype(jnp.int32).reshape(1), lengths, pieces, cosine, sine, keys, values)


def product_kernel(blocks, groups, has_other, has_buffer, order_ref, *refs):
    refs = list(refs)
    row_refs = [refs.pop(0) for _ in range(blocks)]
    weight_refs = [refs.pop(0) for _ in range(4 * groups)]
    bias_ref = refs.pop(0)
    other_ref = refs.pop(0) if has_other else None
    if has_buffer:
        refs.pop(0)
    out_ref, rows_vmem, weights_vmem, total, out_vmem, row_sem, weight_sem, out_sem = refs
    height = row_refs[0].shape[0]
    _, depth = weight_refs[0].shape

    def row_copy(m, j):
        columns = pl.ds(j * depth, depth) if isinstance(j, int) else pl.ds(pl.multiple_of(j * depth, depth), depth)
        return pltpu.make_async_copy(
            row_refs[m].at[:, columns],
            rows_vmem.at[pl.ds(m * height, height), columns],
            row_sem.at[m, j],
        )

    def weight_copy(i):
        return pltpu.make_async_copy(weight_refs[i], weights_vmem.at[i], weight_sem.at[i])

    for j in range(4):
        weight_copy(j).start()
        for m in range(blocks):
            row_copy(m, j).start()
    for i in range(4, 4 * groups):
        weight_copy(i).start()
    total[...] = jnp.zeros_like(total)

    @pl.loop(0, 4 * groups)
    def _(i):
        pltpu.make_async_copy(weight_refs[0], weights_vmem.at[i], weight_sem.at[i]).wait()

        @pl.when(i < 4)
        def _():
            for m in range(blocks):
                row_copy(m, i).wait()

        columns = pl.ds(pl.multiple_of(lax.rem(i, 4) * depth, depth), depth)
        total[i // 4] += lax.dot_general(
            rows_vmem[:, columns],
            weights_vmem[i],
            (((1,), (1,)), ((), ())),
            preferred_element_type=jnp.float32,
        )

    if groups == 1 and not has_other:
        out_ref[...] = (total[0] + bias_ref[...]).astype(jnp.bfloat16)
        return
    low_first = order_ref[blocks] == 1
    if has_other:
        mine = other_ref[...].astype(jnp.float32)
        others = total[0] + bias_ref[...]
    else:
        mine = total[0]
        others = total[1]

    @pl.when(low_first)
    def _():
        out_vmem[...] = jnp.concatenate([mine, others], axis=1).astype(jnp.bfloat16)

    @pl.when(jnp.logical_not(low_first))
    def _():
        out_vmem[...] = jnp.concatenate([others, mine], axis=1).astype(jnp.bfloat16)

    out_copies = [
        pltpu.make_async_copy(out_vmem.at[pl.ds(m * height, height)], out_ref.at[order_ref[m]], out_sem.at[m])
        for m in range(blocks)
    ]
    for copy in out_copies:
        copy.start()
    for copy in out_copies:
        copy.wait()


def product(row_blocks, weights, bias, order, other=None, buffer=None, partial=False):
    blocks = len(row_blocks)
    groups = len(weights) // 4
    height, full = row_blocks[0].shape
    width, depth = weights[0].shape
    anywhere = pl.BlockSpec(memory_space=pl.ANY)
    inside = pl.BlockSpec(memory_space=pltpu.VMEM)
    operands = list(row_blocks) + list(weights) + [bias]
    specs = [anywhere] * (len(operands) - 1) + [inside]
    if other is not None:
        operands.append(other)
        specs.append(inside)
    aliases = {}
    if buffer is not None:
        operands.append(buffer)
        specs.append(anywhere)
        aliases = {len(operands): 0}
    if partial:
        out_shape = jax.ShapeDtypeStruct((blocks * height, width), jnp.bfloat16)
    else:
        out_shape = jax.ShapeDtypeStruct((8, height, 2 * width), jnp.bfloat16)
    return pl.pallas_call(
        functools.partial(product_kernel, blocks, groups, other is not None, buffer is not None),
        out_shape=out_shape,
        grid_spec=pltpu.PrefetchScalarGridSpec(
            num_scalar_prefetch=1,
            grid=(),
            in_specs=specs,
            out_specs=inside if partial else anywhere,
            scratch_shapes=[
                pltpu.VMEM((blocks * height, full), jnp.bfloat16),
                pltpu.VMEM((4 * groups, width, depth), jnp.bfloat16),
                pltpu.VMEM((groups, blocks * height, width), jnp.float32),
                pltpu.VMEM((blocks * height, 2 * width), jnp.bfloat16),
                pltpu.SemaphoreType.DMA((blocks, 4)),
                pltpu.SemaphoreType.DMA((4 * groups,)),
                pltpu.SemaphoreType.DMA((blocks,)),
            ],
        ),
        input_output_aliases=aliases,
        cost_estimate=pl.CostEstimate(
            flops=2 * blocks * height * full * width * groups,
            bytes_accessed=2 * full * width * groups + 2 * blocks * height * full,
            transcendentals=0,
        ),
        name="product",
    )(order, *operands)


def body(qkv_versions, qkv_bias, o_versions, norm_gain, hidden, cache_keys, cache_values, lengths):
    trainer_side = lax.axis_index("role") == 0
    shard_index = lax.axis_index("shard")
    rep_index = lax.axis_index("rep")
    rep_total = lax.axis_size("rep")
    own_qkv = qkv_versions[0].T
    own_out = o_versions[0]
    states = hidden[0].astype(jnp.float32)
    rows = states.shape[0]
    tokens = rows * STEPS
    near, far, low_first = owner_order(shard_index)
    normed = normalize(states, norm_gain[0]).reshape(tokens, D)
    qkv_slots = gather_weights(own_qkv)
    width = own_qkv.shape[0]
    bias = qkv_bias[0].astype(jnp.float32).reshape(1, -1)
    own_bias = lax.dynamic_slice_in_dim(bias, shard_index * width, width, 1)
    pair_bias = lax.dynamic_slice_in_dim(bias, (shard_index ^ 1) * width, width, 1)
    same, mirror = gather_rows(slot_columns(normed, rep_index))
    order = jnp.concatenate([near, far, low_first])
    spread = lax.all_to_all(own_out, "shard", split_axis=0, concat_axis=1, tiled=True)
    turned = rotate_columns(after(spread, same[3]))
    mine = product(same + mirror, qkv_slots[0], own_bias, after(order, turned), partial=True)
    part = product(same + mirror, qkv_slots[1], pair_bias, order, other=mine)
    packed = to_owners(part)
    folded_qkv = rotate_column_part(
        after(jnp.concatenate(qkv_slots[0], axis=1), part), rep_index, rep_total
    )
    out_slots = gather_weights(after(own_out.T, qkv_slots[1][2]))
    weights = out_slots[0] + out_slots[1]
    folded_out = lax.all_to_all(
        after(turned, part), "shard", split_axis=1, concat_axis=0, tiled=True
    )
    packed = after(packed, folded_qkv, *weights)
    attended = attend_slots(packed, cache_keys[0], cache_values[0], lengths[0], rep_index)
    same, mirror = gather_rows(attended)
    no_bias = jnp.zeros((1, own_out.shape[1]), jnp.float32)
    part = product(same, weights, no_bias, jnp.concatenate([near, low_first]))
    part = product(mirror, weights, no_bias, jnp.concatenate([far, low_first]), buffer=part)
    projected = to_owners(part)
    projected = projected.transpose(1, 0, 2).reshape(rows, STEPS, D).astype(jnp.float32)
    layer_out = (states + projected).astype(jnp.bfloat16)[None]
    sent_qkv = shifted(folded_qkv, "role", 1)
    sent_out = shifted(folded_out, "role", 1)
    new_qkv = jnp.where(trainer_side, folded_qkv, sent_qkv)
    new_o = jnp.where(trainer_side, folded_out, sent_out)
    return (layer_out, new_qkv.T[None], new_o[None])


def solution(mesh):
    in_specs = (
        P("role", "rep", "shard"),
        P("role", None),
        P("role", "rep", "shard"),
        P("role", None),
        P("role", ("shard", "rep"), None, None),
        P("role", ("shard", "rep"), None, None),
        P("role", ("shard", "rep"), None, None),
        P("role", ("shard", "rep")),
    )
    out_specs = (
        P("role", ("shard", "rep"), None, None),
        P("role", "rep", "shard"),
        P("role", "rep", "shard"),
    )
    return jax.shard_map(body, mesh=mesh, in_specs=in_specs, out_specs=out_specs, check_vma=False)
```

```python
import functools
import math

import jax
import jax.numpy as jnp
from jax import lax
from jax.experimental import pallas as pl
from jax.experimental.pallas import tpu as pltpu
from jax.sharding import PartitionSpec as P


FACTOR_A = 40
FACTOR_B = 128
D = 5120
HEADS = 40
KV_HEADS = 8
HEAD_DIM = 128
QDIM = 5120
KVD = 1024
STEPS = 4


EPSILON = 1e-06
ROPE_BASE = 1000000.0


LINES = 4


def shifted(value, axis, steps):
    count = lax.axis_size(axis)
    initial, last = (max(0, -steps), min(count, count - steps))
    return lax.ppermute(value, axis, [(source, source + steps) for source in range(initial, last)])


def along_z(value, steps):
    count = lax.axis_size("shard")
    pairs = [(s, (s + steps * LINES) % count) for s in range(count)]
    return lax.ppermute(value, "shard", pairs)


def mirror_y(value):
    count = lax.axis_size("shard")
    return lax.ppermute(value, "shard", [(s, s ^ 3) for s in range(count)])


def next_y(value):
    count = lax.axis_size("shard")
    return lax.ppermute(value, "shard", [(s, s ^ 1) for s in range(count)])


def other_chip(value):
    return lax.ppermute(value, "rep", [(r, r ^ 2) for r in range(4)])


def other_core(value):
    return lax.ppermute(value, "rep", [(r, r ^ 1) for r in range(4)])


def crossed(even_value, odd_value, even_pair, odd_pair):
    value = jnp.where(lax.axis_index("rep") % 2 == 0, even_value, odd_value)
    reps = lax.axis_size("rep")
    pairs = []
    for s in range(lax.axis_size("shard")):
        for r in range(reps):
            to_shard, to_rep = (even_pair if r % 2 == 0 else odd_pair)(s, r)
            pairs.append((s * reps + r, to_shard * reps + to_rep))
    return lax.ppermute(value, ("shard", "rep"), pairs)


def gather_rows(own):
    count = lax.axis_size("shard")
    below = along_z(own, 1)
    above = along_z(own, -1)
    mirror = mirror_y(own)
    far = crossed(
        below,
        above,
        lambda s, r: ((s + LINES) % count, r),
        lambda s, r: ((s - LINES) % count, r),
    )
    mirror, _ = lax.optimization_barrier((mirror, far))
    mirror_below = along_z(mirror, 1)
    mirror_above = along_z(mirror, -1)
    mirror_far = mirror_y(far)
    return ((own, below, above, far), (mirror, mirror_below, mirror_above, mirror_far))


def gather_weights(own, gate=None, late=None):
    across = other_chip(own)
    pair = next_y(own)
    if gate is not None:
        across, pair, _ = lax.optimization_barrier((across, pair, gate))
    beside = other_core(own)
    pair_beside = other_core(pair)
    across_beside = other_core(across)
    pair_across = crossed(
        pair, across, lambda s, r: (s, r ^ 2), lambda s, r: (s ^ 1, r)
    )
    crossing = pair_across
    if late is not None:
        pair_across = after(pair_across, late)
    pair_across_beside = other_core(pair_across)
    return (
        (own, beside, across, across_beside),
        (pair, pair_beside, pair_across, pair_across_beside),
        crossing,
    )


def after(value, *others):
    return lax.optimization_barrier((value,) + others)[0]


def slot_columns(rows, rep_index):
    width = rows.shape[1] // 4
    return jnp.concatenate(
        [lax.dynamic_slice_in_dim(rows, (rep_index ^ j) * width, width, 1) for j in range(4)], axis=1
    )


def owner_order(shard_index):
    line_z = shard_index // LINES
    high = (shard_index // 2) % 2
    steps = jnp.array([0, -1, 1, 2], jnp.int32)
    owners = jnp.mod(line_z + steps, 4) * 2
    low_first = (1 - shard_index % 2).reshape(1)
    return owners + high, owners + 1 - high, low_first.astype(jnp.int32)


def to_owners(ordered):
    lines = lax.axis_size("shard") // LINES
    groups = [
        [z * LINES + y for z in range(lines) for y in (0, 3)],
        [z * LINES + y for z in range(lines) for y in (1, 2)],
    ]
    return lax.all_to_all(
        ordered, "shard", split_axis=0, concat_axis=0, axis_index_groups=groups, tiled=True
    )


def hadamard_pair():
    modulus = FACTOR_A // 2 - 1
    residues = jnp.arange(modulus, dtype=jnp.int32)
    squares = jnp.arange(1, modulus, dtype=jnp.int32) ** 2 % modulus
    differ = (residues[None, :] - residues[:, None]) % modulus
    residue_mask = jnp.any(differ[:, :, None] == squares[None, None, :], axis=2)
    jacobs = jnp.where(differ == 0, 0.0, jnp.where(residue_mask, 1.0, -1.0)).astype(jnp.float32)
    top_row = jnp.concatenate(
        [jnp.zeros((1, 1), jnp.float32), jnp.ones((1, modulus), jnp.float32)], axis=1
    )
    lower_rows = jnp.concatenate([-jnp.ones((modulus, 1), jnp.float32), jacobs], axis=1)
    paley_core = jnp.eye(modulus + 1, dtype=jnp.float32) + jnp.concatenate(
        [top_row, lower_rows], axis=0
    )
    doubler = jnp.array([[1.0, 1.0], [1.0, -1.0]], jnp.float32)
    outer_factor = jnp.kron(doubler, paley_core)
    indices = jnp.arange(FACTOR_B, dtype=jnp.int32)
    common_bits = indices[:, None] & indices[None, :]
    parity = jnp.zeros((FACTOR_B, FACTOR_B), jnp.int32)
    for bit_level in range(FACTOR_B.bit_length() - 1):
        parity = parity + (common_bits >> bit_level & 1)
    inner_factor = (1 - 2 * (parity % 2)).astype(jnp.float32)
    return (outer_factor, inner_factor)


def fold_kernel(outer_ref, inner_ref, *refs):
    slot_refs, out_ref = refs[:4], refs[4]
    parts = out_ref.shape[1] // FACTOR_B
    sign = (outer_ref[0, 0] * outer_ref[2 * parts, 0]).astype(jnp.bfloat16)
    inner = inner_ref[...]
    stacked = jnp.concatenate([inner, inner * sign], axis=0)
    height = 32

    @pl.loop(0, out_ref.shape[0] // height)
    def _(step):
        span = pl.ds(pl.multiple_of(step * height, height), height)
        totals = [jnp.zeros((height, FACTOR_B), jnp.float32) for _ in range(parts)]
        for slot in range(2):
            for i in range(parts):
                lanes = slice(i * FACTOR_B, (i + 1) * FACTOR_B)
                both = jnp.concatenate(
                    [slot_refs[slot][span, lanes], slot_refs[slot + 2][span, lanes]], axis=1
                )
                mixed = jnp.dot(both, stacked, preferred_element_type=jnp.float32)
                for x in range(parts):
                    totals[x] = totals[x] + outer_ref[slot * parts + i, x] * mixed
        for x in range(parts):
            out_ref[span, x * FACTOR_B : (x + 1) * FACTOR_B] = (
                totals[x] * (1.0 / math.sqrt(D))
            ).astype(jnp.bfloat16)


def rotate_column_part(slots, part_index, part_total):
    outer_factor, inner_factor = hadamard_pair()
    height, width = slots[0].shape
    part_width = FACTOR_A // part_total
    outer_part = lax.dynamic_slice_in_dim(outer_factor, part_index * part_width, part_width, 1)
    outer_part = jnp.concatenate(
        [
            lax.dynamic_slice_in_dim(outer_part, (part_index ^ j) * part_width, part_width, 0)
            for j in range(part_total)
        ],
        axis=0,
    )
    rows = 64
    block = pl.BlockSpec((rows, width), lambda i: (i, 0))
    return pl.pallas_call(
        fold_kernel,
        out_shape=jax.ShapeDtypeStruct((height, width), jnp.bfloat16),
        grid=(height // rows,),
        in_specs=[
            pl.BlockSpec(memory_space=pltpu.SMEM),
            pl.BlockSpec((FACTOR_B, FACTOR_B), lambda i: (0, 0)),
        ]
        + [block] * 4,
        out_specs=block,
        cost_estimate=pl.CostEstimate(flops=4_000_000_000, bytes_accessed=6_000_000, transcendentals=0),
        name="fold_part",
    )(outer_part, inner_factor.astype(jnp.bfloat16), *slots)


def rotate_columns(matrix):
    outer_factor, inner_factor = hadamard_pair()
    height = matrix.shape[0]
    blocks = matrix.reshape(height, FACTOR_A, FACTOR_B)
    inner_mixed = jnp.einsum(
        "mab,by->may", blocks, inner_factor.astype(jnp.bfloat16), preferred_element_type=jnp.float32
    )
    turned = jnp.einsum("may,ax->mxy", inner_mixed, outer_factor, precision=lax.Precision.HIGHEST)
    return (turned.reshape(height, D) * (1.0 / math.sqrt(D))).astype(jnp.bfloat16)


def normalize(states, gain):
    mean_square = jnp.mean(states * states, axis=-1, keepdims=True)
    return (states * lax.rsqrt(mean_square + EPSILON) * gain.astype(jnp.float32)).astype(
        jnp.bfloat16
    )


def spun(vectors, cosine, sine):
    return vectors * cosine + pltpu.roll(vectors, HEAD_DIM // 2, 1) * sine


def attention_kernel(
    part_ref, length_ref, packed_ref, cosine_ref, sine_ref, keys_ref, values_ref, out_ref, spun_ref, sum_ref
):
    block = pl.program_id(0)
    group = part_ref[0] ^ pl.program_id(1)
    cached = keys_ref.shape[1]
    rows = keys_ref.shape[0]
    tokens = rows * STEPS
    piece_heads = packed_ref.shape[2] // HEAD_DIM
    ratio = HEADS // KV_HEADS
    cosine = cosine_ref[...]
    sine = sine_ref[...]

    def head(index):
        offset = pl.multiple_of(lax.rem(index, piece_heads) * HEAD_DIM, HEAD_DIM)
        return packed_ref[index // piece_heads, :, pl.ds(offset, HEAD_DIM)]

    for u in range(2 * ratio):
        turned = spun(head(group * 2 * ratio + u).astype(jnp.float32), cosine, sine)
        spun_ref[:, u * HEAD_DIM : (u + 1) * HEAD_DIM] = turned.astype(jnp.bfloat16).astype(jnp.float32)
    scale = 1.0 / math.sqrt(HEAD_DIM)
    pairs = rows // 2
    group_rows = 2 * STEPS * ratio
    count = pairs * group_rows
    place = lax.broadcasted_iota(jnp.int32, (count, 1), 0)
    token_of = (place // group_rows) * (2 * STEPS) + place % (2 * STEPS)
    row_of = token_of // STEPS
    live = jnp.zeros((count, 1), jnp.int32)
    for row in range(rows):
        live = jnp.where(row_of == row, length_ref[block * rows + row], live)
    old_start = (row_of % 2) * cached
    old_column = lax.broadcasted_iota(jnp.int32, (count, 2 * cached), 1) - old_start
    old_kept = (old_column >= 0) & (old_column < live)
    new_column = lax.broadcasted_iota(jnp.int32, (count, tokens), 1)
    new_kept = (new_column >= row_of * STEPS) & (new_column <= token_of)
    contract_last = (((1,), (1,)), ((), ()))

    def columns(half, u):
        return slice((half * ratio + u) * HEAD_DIM, (half * ratio + u + 1) * HEAD_DIM)

    for half in range(2):
        lanes = slice(half * HEAD_DIM, (half + 1) * HEAD_DIM)
        new_keys = spun(head(HEADS + group * 2 + half).astype(jnp.float32), cosine, sine).astype(jnp.bfloat16)
        new_values = head(HEADS + KV_HEADS + group * 2 + half)
        queries = [
            jnp.concatenate(
                [spun_ref[2 * STEPS * pair : 2 * STEPS * (pair + 1), columns(half, u)] for u in range(ratio)],
                axis=0,
            )
            for pair in range(pairs)
        ]
        old_scores = jnp.concatenate(
            [
                lax.dot_general(
                    queries[pair].astype(jnp.bfloat16),
                    keys_ref[2 * pair : 2 * pair + 2, :, lanes].reshape(2 * cached, HEAD_DIM),
                    contract_last,
                    preferred_element_type=jnp.float32,
                )
                for pair in range(pairs)
            ],
            axis=0,
        )
        new_scores = lax.dot_general(
            jnp.concatenate(queries, axis=0).astype(jnp.bfloat16),
            new_keys,
            contract_last,
            preferred_element_type=jnp.float32,
        )
        old_scores = jnp.where(old_kept, old_scores * scale, -1e30)
        new_scores = jnp.where(new_kept, new_scores * scale, -1e30)
        peak = jnp.maximum(
            jnp.max(old_scores, axis=1, keepdims=True), jnp.max(new_scores, axis=1, keepdims=True)
        )
        old_exp = jnp.exp(old_scores - peak)
        new_exp = jnp.exp(new_scores - peak)
        share = 1.0 / (jnp.sum(old_exp, axis=1, keepdims=True) + jnp.sum(new_exp, axis=1, keepdims=True))
        old_weights = old_exp * share
        fresh = jnp.dot(
            (new_exp * share).astype(jnp.bfloat16), new_values, preferred_element_type=jnp.float32
        )
        for pair in range(pairs):
            part = slice(pair * group_rows, (pair + 1) * group_rows)
            total = fresh[part] + jnp.dot(
                old_weights[part].astype(jnp.bfloat16),
                values_ref[2 * pair : 2 * pair + 2, :, lanes].reshape(2 * cached, HEAD_DIM),
                preferred_element_type=jnp.float32,
            )
            for u in range(ratio):
                sum_ref[2 * STEPS * pair : 2 * STEPS * (pair + 1), columns(half, u)] = total[
                    2 * STEPS * u : 2 * STEPS * (u + 1)
                ]
    out_ref[...] = sum_ref[...].astype(jnp.bfloat16)


def attend_slots(pieces, keys, values, lengths, rep_index):
    rows, cached = keys.shape[0], keys.shape[1]
    block_rows = 8
    tokens = block_rows * STEPS
    positions = (lengths[:, None] + jnp.arange(STEPS, dtype=jnp.int32)[None, :]).reshape(-1)
    frequency = jnp.power(
        jnp.float32(ROPE_BASE), -jnp.arange(0, HEAD_DIM, 2, dtype=jnp.float32) / HEAD_DIM
    )
    angles = positions.astype(jnp.float32)[:, None] * frequency[None, :]
    cosine, sine = jnp.cos(angles), jnp.sin(angles)
    cosine = jnp.concatenate([cosine, cosine], axis=1)
    sine = jnp.concatenate([-sine, sine], axis=1)
    width = QDIM // 4
    pair_width = KVD // 4
    return pl.pallas_call(
        attention_kernel,
        out_shape=jax.ShapeDtypeStruct((rows * STEPS, QDIM), jnp.bfloat16),
        grid_spec=pltpu.PrefetchScalarGridSpec(
            num_scalar_prefetch=2,
            grid=(rows // block_rows, 4),
            in_specs=[
                pl.BlockSpec((pieces.shape[0], tokens, pieces.shape[2]), lambda i, j, p, n: (0, i, 0)),
                pl.BlockSpec((tokens, HEAD_DIM), lambda i, j, p, n: (i, 0)),
                pl.BlockSpec((tokens, HEAD_DIM), lambda i, j, p, n: (i, 0)),
                pl.BlockSpec((block_rows, cached, pair_width), lambda i, j, p, n: (i, 0, p[0] ^ j)),
                pl.BlockSpec((block_rows, cached, pair_width), lambda i, j, p, n: (i, 0, p[0] ^ j)),
            ],
            out_specs=pl.BlockSpec((tokens, width), lambda i, j, p, n: (i, j)),
            scratch_shapes=[
                pltpu.VMEM((tokens, width), jnp.float32),
                pltpu.VMEM((tokens, width), jnp.float32),
            ],
        ),
        cost_estimate=pl.CostEstimate(flops=2_000_000_000, bytes_accessed=10_000_000, transcendentals=2_000_000),
        name="attend_slots",
    )(rep_index.astype(jnp.int32).reshape(1), lengths, pieces, cosine, sine, keys, values)


def product_kernel(blocks, groups, has_buffer, order_ref, *refs):
    refs = list(refs)
    row_refs = [refs.pop(0) for _ in range(blocks)]
    weight_refs = [refs.pop(0) for _ in range(4 * groups)]
    bias_ref = refs.pop(0)
    if has_buffer:
        refs.pop(0)
    out_ref, rows_vmem, weights_vmem, total, out_vmem, row_sem, weight_sem, out_sem = refs
    height = row_refs[0].shape[0]
    _, depth = weight_refs[0].shape

    def row_copy(m, j):
        columns = pl.ds(j * depth, depth) if isinstance(j, int) else pl.ds(pl.multiple_of(j * depth, depth), depth)
        return pltpu.make_async_copy(
            row_refs[m].at[:, columns],
            rows_vmem.at[pl.ds(m * height, height), columns],
            row_sem.at[m, j],
        )

    def weight_copy(i):
        return pltpu.make_async_copy(weight_refs[i], weights_vmem.at[i], weight_sem.at[i])

    for j in range(4):
        weight_copy(j).start()
        for m in range(blocks):
            row_copy(m, j).start()
    for i in range(4, 4 * groups):
        weight_copy(i).start()
    total[...] = jnp.zeros_like(total)

    @pl.loop(0, 4 * groups)
    def _(i):
        pltpu.make_async_copy(weight_refs[0], weights_vmem.at[i], weight_sem.at[i]).wait()

        @pl.when(i < 4)
        def _():
            for m in range(blocks):
                row_copy(m, i).wait()

        columns = pl.ds(pl.multiple_of(lax.rem(i, 4) * depth, depth), depth)
        total[i // 4] += lax.dot_general(
            rows_vmem[:, columns],
            weights_vmem[i],
            (((1,), (1,)), ((), ())),
            preferred_element_type=jnp.float32,
        )

    low_first = order_ref[blocks] == 1
    mine = total[0] + bias_ref[0:1]
    others = total[1] + bias_ref[1:2]

    @pl.when(low_first)
    def _():
        out_vmem[...] = jnp.concatenate([mine, others], axis=1).astype(jnp.bfloat16)

    @pl.when(jnp.logical_not(low_first))
    def _():
        out_vmem[...] = jnp.concatenate([others, mine], axis=1).astype(jnp.bfloat16)

    out_copies = [
        pltpu.make_async_copy(out_vmem.at[pl.ds(m * height, height)], out_ref.at[order_ref[m]], out_sem.at[m])
        for m in range(blocks)
    ]
    for copy in out_copies:
        copy.start()
    for copy in out_copies:
        copy.wait()


def product(row_blocks, weights, bias, order, buffer=None):
    blocks = len(row_blocks)
    groups = len(weights) // 4
    height, full = row_blocks[0].shape
    width, depth = weights[0].shape
    anywhere = pl.BlockSpec(memory_space=pl.ANY)
    inside = pl.BlockSpec(memory_space=pltpu.VMEM)
    operands = list(row_blocks) + list(weights) + [bias]
    specs = [anywhere] * (len(operands) - 1) + [inside]
    aliases = {}
    if buffer is not None:
        operands.append(buffer)
        specs.append(anywhere)
        aliases = {len(operands): 0}
    out_shape = jax.ShapeDtypeStruct((8, height, 2 * width), jnp.bfloat16)
    return pl.pallas_call(
        functools.partial(product_kernel, blocks, groups, buffer is not None),
        out_shape=out_shape,
        grid_spec=pltpu.PrefetchScalarGridSpec(
            num_scalar_prefetch=1,
            grid=(),
            in_specs=specs,
            out_specs=anywhere,
            scratch_shapes=[
                pltpu.VMEM((blocks * height, full), jnp.bfloat16),
                pltpu.VMEM((4 * groups, width, depth), jnp.bfloat16),
                pltpu.VMEM((groups, blocks * height, width), jnp.float32),
                pltpu.VMEM((blocks * height, 2 * width), jnp.bfloat16),
                pltpu.SemaphoreType.DMA((blocks, 4)),
                pltpu.SemaphoreType.DMA((4 * groups,)),
                pltpu.SemaphoreType.DMA((blocks,)),
            ],
        ),
        input_output_aliases=aliases,
        cost_estimate=pl.CostEstimate(
            flops=2 * blocks * height * full * width * groups,
            bytes_accessed=2 * full * width * groups + 2 * blocks * height * full,
            transcendentals=0,
        ),
        name="product",
    )(order, *operands)


def body(qkv_versions, qkv_bias, o_versions, norm_gain, hidden, cache_keys, cache_values, lengths):
    trainer_side = lax.axis_index("role") == 0
    shard_index = lax.axis_index("shard")
    rep_index = lax.axis_index("rep")
    rep_total = lax.axis_size("rep")
    own_qkv = qkv_versions[0].T
    own_out = o_versions[0]
    states = hidden[0].astype(jnp.float32)
    rows = states.shape[0]
    tokens = rows * STEPS
    near, far, low_first = owner_order(shard_index)
    normed = normalize(states, norm_gain[0]).reshape(tokens, D)
    qkv_slots = gather_weights(own_qkv)
    width = own_qkv.shape[0]
    bias = qkv_bias[0].astype(jnp.float32).reshape(1, -1)
    own_bias = lax.dynamic_slice_in_dim(bias, shard_index * width, width, 1)
    pair_bias = lax.dynamic_slice_in_dim(bias, (shard_index ^ 1) * width, width, 1)
    same, mirror = gather_rows(slot_columns(normed, rep_index))
    order = jnp.concatenate([near, far, low_first])
    spread = lax.all_to_all(own_out, "shard", split_axis=0, concat_axis=1, tiled=True)
    turned = rotate_columns(after(spread, same[3]))
    folded_out = lax.all_to_all(
        turned, "shard", split_axis=1, concat_axis=0, tiled=True
    )
    both_bias = jnp.concatenate([own_bias, pair_bias], axis=0)
    part = product(
        same + mirror, qkv_slots[0] + qkv_slots[1], both_bias, after(order, turned)
    )
    packed = to_owners(after(part, folded_out))
    out_slots = gather_weights(after(own_out.T, turned), part, packed)
    weights = out_slots[0] + out_slots[1]
    sent_out = shifted(after(folded_out, part), "role", 1)
    packed = after(packed, out_slots[2], *weights[:6])
    attended = attend_slots(packed, cache_keys[0], cache_values[0], lengths[0], rep_index)
    folded_qkv = rotate_column_part(
        (after(qkv_slots[0][0], attended),) + qkv_slots[0][1:], rep_index, rep_total
    )
    sent_qkv = shifted(folded_qkv, "role", 1)
    same, mirror = gather_rows(attended)
    no_bias = jnp.zeros((2, own_out.shape[1]), jnp.float32)
    part = product(same, weights, no_bias, jnp.concatenate([near, low_first]))
    part = product(mirror, weights, no_bias, jnp.concatenate([far, low_first]), buffer=part)
    sent_qkv, sent_out = after(sent_qkv, part), after(sent_out, part)
    projected = to_owners(part)
    projected = projected.transpose(1, 0, 2).reshape(rows, STEPS, D).astype(jnp.float32)
    layer_out = (states + projected).astype(jnp.bfloat16)[None]
    new_qkv = jnp.where(trainer_side, folded_qkv, sent_qkv)
    new_o = jnp.where(trainer_side, folded_out, sent_out)
    return (layer_out, new_qkv.T[None], new_o[None])


def solution(mesh):
    in_specs = (
        P("role", "rep", "shard"),
        P("role", None),
        P("role", "rep", "shard"),
        P("role", None),
        P("role", ("shard", "rep"), None, None),
        P("role", ("shard", "rep"), None, None),
        P("role", ("shard", "rep"), None, None),
        P("role", ("shard", "rep")),
    )
    out_specs = (
        P("role", ("shard", "rep"), None, None),
        P("role", "rep", "shard"),
        P("role", "rep", "shard"),
    )
    return jax.shard_map(body, mesh=mesh, in_specs=in_specs, out_specs=out_specs, check_vma=False)
```

```python
import functools
import math

import jax
import jax.numpy as jnp
from jax import lax
from jax.experimental import pallas as pl
from jax.experimental.pallas import tpu as pltpu
from jax.sharding import PartitionSpec as P


FACTOR_A = 40
FACTOR_B = 128
D = 5120
HEADS = 40
KV_HEADS = 8
HEAD_DIM = 128
QDIM = 5120
KVD = 1024
STEPS = 4


EPSILON = 1e-06
ROPE_BASE = 1000000.0


LINES = 4


def shifted(value, axis, steps):
    count = lax.axis_size(axis)
    initial, last = (max(0, -steps), min(count, count - steps))
    return lax.ppermute(value, axis, [(source, source + steps) for source in range(initial, last)])


def along_z(value, steps):
    count = lax.axis_size("shard")
    pairs = [(s, (s + steps * LINES) % count) for s in range(count)]
    return lax.ppermute(value, "shard", pairs)


def mirror_y(value):
    count = lax.axis_size("shard")
    return lax.ppermute(value, "shard", [(s, s ^ 3) for s in range(count)])


def next_y(value):
    count = lax.axis_size("shard")
    return lax.ppermute(value, "shard", [(s, s ^ 1) for s in range(count)])


def other_chip(value):
    return lax.ppermute(value, "rep", [(r, r ^ 2) for r in range(4)])


def other_core(value):
    return lax.ppermute(value, "rep", [(r, r ^ 1) for r in range(4)])


def crossed(even_value, odd_value, even_pair, odd_pair):
    value = jnp.where(lax.axis_index("rep") % 2 == 0, even_value, odd_value)
    reps = lax.axis_size("rep")
    pairs = []
    for s in range(lax.axis_size("shard")):
        for r in range(reps):
            to_shard, to_rep = (even_pair if r % 2 == 0 else odd_pair)(s, r)
            pairs.append((s * reps + r, to_shard * reps + to_rep))
    return lax.ppermute(value, ("shard", "rep"), pairs)


def gather_rows(own):
    count = lax.axis_size("shard")
    below = along_z(own, 1)
    above = along_z(own, -1)
    mirror = mirror_y(own)
    far = crossed(
        below,
        above,
        lambda s, r: ((s + LINES) % count, r),
        lambda s, r: ((s - LINES) % count, r),
    )
    mirror, _ = lax.optimization_barrier((mirror, far))
    mirror_below = along_z(mirror, 1)
    mirror_above = along_z(mirror, -1)
    mirror_far = mirror_y(far)
    return ((own, below, above, far), (mirror, mirror_below, mirror_above, mirror_far))


def gather_weights(own, gate=None, late=None):
    across = other_chip(own)
    pair = next_y(own)
    if gate is not None:
        across, pair, _ = lax.optimization_barrier((across, pair, gate))
    beside = other_core(own)
    pair_beside = other_core(pair)
    across_beside = other_core(across)
    pair_across = crossed(
        pair, across, lambda s, r: (s, r ^ 2), lambda s, r: (s ^ 1, r)
    )
    crossing = pair_across
    if late is not None:
        pair_across = after(pair_across, late)
    pair_across_beside = other_core(pair_across)
    return (
        (own, beside, across, across_beside),
        (pair, pair_beside, pair_across, pair_across_beside),
        crossing,
    )


def after(value, *others):
    return lax.optimization_barrier((value,) + others)[0]


def slot_columns(rows, rep_index):
    width = rows.shape[1] // 4
    return jnp.concatenate(
        [lax.dynamic_slice_in_dim(rows, (rep_index ^ j) * width, width, 1) for j in range(4)], axis=1
    )


def owner_order(shard_index):
    line_z = shard_index // LINES
    high = (shard_index // 2) % 2
    steps = jnp.array([0, -1, 1, 2], jnp.int32)
    owners = jnp.mod(line_z + steps, 4) * 2
    low_first = (1 - shard_index % 2).reshape(1)
    return owners + high, owners + 1 - high, low_first.astype(jnp.int32)


def to_owners(ordered):
    lines = lax.axis_size("shard") // LINES
    groups = [
        [z * LINES + y for z in range(lines) for y in (0, 3)],
        [z * LINES + y for z in range(lines) for y in (1, 2)],
    ]
    return lax.all_to_all(
        ordered, "shard", split_axis=0, concat_axis=0, axis_index_groups=groups, tiled=True
    )


def hadamard_pair():
    modulus = FACTOR_A // 2 - 1
    residues = jnp.arange(modulus, dtype=jnp.int32)
    squares = jnp.arange(1, modulus, dtype=jnp.int32) ** 2 % modulus
    differ = (residues[None, :] - residues[:, None]) % modulus
    residue_mask = jnp.any(differ[:, :, None] == squares[None, None, :], axis=2)
    jacobs = jnp.where(differ == 0, 0.0, jnp.where(residue_mask, 1.0, -1.0)).astype(jnp.float32)
    top_row = jnp.concatenate(
        [jnp.zeros((1, 1), jnp.float32), jnp.ones((1, modulus), jnp.float32)], axis=1
    )
    lower_rows = jnp.concatenate([-jnp.ones((modulus, 1), jnp.float32), jacobs], axis=1)
    paley_core = jnp.eye(modulus + 1, dtype=jnp.float32) + jnp.concatenate(
        [top_row, lower_rows], axis=0
    )
    doubler = jnp.array([[1.0, 1.0], [1.0, -1.0]], jnp.float32)
    outer_factor = jnp.kron(doubler, paley_core)
    indices = jnp.arange(FACTOR_B, dtype=jnp.int32)
    common_bits = indices[:, None] & indices[None, :]
    parity = jnp.zeros((FACTOR_B, FACTOR_B), jnp.int32)
    for bit_level in range(FACTOR_B.bit_length() - 1):
        parity = parity + (common_bits >> bit_level & 1)
    inner_factor = (1 - 2 * (parity % 2)).astype(jnp.float32)
    return (outer_factor, inner_factor)


def fold_kernel(outer_ref, inner_ref, *refs):
    slot_refs, out_ref = refs[:4], refs[4]
    parts = out_ref.shape[1] // FACTOR_B
    sign = (outer_ref[0, 0] * outer_ref[2 * parts, 0]).astype(jnp.bfloat16)
    inner = inner_ref[...]
    stacked = jnp.concatenate([inner, inner * sign], axis=0)
    height = 32

    @pl.loop(0, out_ref.shape[0] // height)
    def _(step):
        span = pl.ds(pl.multiple_of(step * height, height), height)
        totals = [jnp.zeros((height, FACTOR_B), jnp.float32) for _ in range(parts)]
        for slot in range(2):
            for i in range(parts):
                lanes = slice(i * FACTOR_B, (i + 1) * FACTOR_B)
                both = jnp.concatenate(
                    [slot_refs[slot][span, lanes], slot_refs[slot + 2][span, lanes]], axis=1
                )
                mixed = jnp.dot(both, stacked, preferred_element_type=jnp.float32)
                for x in range(parts):
                    totals[x] = totals[x] + outer_ref[slot * parts + i, x] * mixed
        for x in range(parts):
            out_ref[span, x * FACTOR_B : (x + 1) * FACTOR_B] = (
                totals[x] * (1.0 / math.sqrt(D))
            ).astype(jnp.bfloat16)


def rotate_column_part(slots, part_index, part_total):
    outer_factor, inner_factor = hadamard_pair()
    height, width = slots[0].shape
    part_width = FACTOR_A // part_total
    outer_part = lax.dynamic_slice_in_dim(outer_factor, part_index * part_width, part_width, 1)
    outer_part = jnp.concatenate(
        [
            lax.dynamic_slice_in_dim(outer_part, (part_index ^ j) * part_width, part_width, 0)
            for j in range(part_total)
        ],
        axis=0,
    )
    rows = 64
    block = pl.BlockSpec((rows, width), lambda i: (i, 0))
    return pl.pallas_call(
        fold_kernel,
        out_shape=jax.ShapeDtypeStruct((height, width), jnp.bfloat16),
        grid=(height // rows,),
        in_specs=[
            pl.BlockSpec(memory_space=pltpu.SMEM),
            pl.BlockSpec((FACTOR_B, FACTOR_B), lambda i: (0, 0)),
        ]
        + [block] * 4,
        out_specs=block,
        cost_estimate=pl.CostEstimate(flops=4_000_000_000, bytes_accessed=6_000_000, transcendentals=0),
        name="fold_part",
    )(outer_part, inner_factor.astype(jnp.bfloat16), *slots)


def rotate_columns(matrix):
    outer_factor, inner_factor = hadamard_pair()
    height = matrix.shape[0]
    blocks = matrix.reshape(height, FACTOR_A, FACTOR_B)
    inner_mixed = jnp.einsum(
        "mab,by->may", blocks, inner_factor.astype(jnp.bfloat16), preferred_element_type=jnp.float32
    )
    turned = jnp.einsum("may,ax->mxy", inner_mixed, outer_factor, precision=lax.Precision.HIGHEST)
    return (turned.reshape(height, D) * (1.0 / math.sqrt(D))).astype(jnp.bfloat16)


def normalize(states, gain):
    mean_square = jnp.mean(states * states, axis=-1, keepdims=True)
    return (states * lax.rsqrt(mean_square + EPSILON) * gain.astype(jnp.float32)).astype(
        jnp.bfloat16
    )


def spun(vectors, cosine, sine):
    return vectors * cosine + pltpu.roll(vectors, HEAD_DIM // 2, 1) * sine


def attention_kernel(
    part_ref, length_ref, packed_ref, cosine_ref, sine_ref, keys_ref, values_ref, out_ref, spun_ref, sum_ref
):
    block = pl.program_id(0)
    group = part_ref[0] ^ pl.program_id(1)
    cached = keys_ref.shape[1]
    rows = keys_ref.shape[0]
    tokens = rows * STEPS
    piece_heads = packed_ref.shape[2] // HEAD_DIM
    ratio = HEADS // KV_HEADS
    cosine = cosine_ref[...]
    sine = sine_ref[...]

    def head(index):
        offset = pl.multiple_of(lax.rem(index, piece_heads) * HEAD_DIM, HEAD_DIM)
        return packed_ref[index // piece_heads, :, pl.ds(offset, HEAD_DIM)]

    for u in range(2 * ratio):
        turned = spun(head(group * 2 * ratio + u).astype(jnp.float32), cosine, sine)
        spun_ref[:, u * HEAD_DIM : (u + 1) * HEAD_DIM] = turned.astype(jnp.bfloat16).astype(jnp.float32)
    scale = 1.0 / math.sqrt(HEAD_DIM)
    pairs = rows // 2
    group_rows = 2 * STEPS * ratio
    count = pairs * group_rows
    place = lax.broadcasted_iota(jnp.int32, (count, 1), 0)
    token_of = (place // group_rows) * (2 * STEPS) + place % (2 * STEPS)
    row_of = token_of // STEPS
    live = jnp.zeros((count, 1), jnp.int32)
    for row in range(rows):
        live = jnp.where(row_of == row, length_ref[block * rows + row], live)
    old_start = (row_of % 2) * cached
    old_column = lax.broadcasted_iota(jnp.int32, (count, 2 * cached), 1) - old_start
    old_kept = (old_column >= 0) & (old_column < live)
    new_column = lax.broadcasted_iota(jnp.int32, (count, tokens), 1)
    new_kept = (new_column >= row_of * STEPS) & (new_column <= token_of)
    contract_last = (((1,), (1,)), ((), ()))

    def columns(half, u):
        return slice((half * ratio + u) * HEAD_DIM, (half * ratio + u + 1) * HEAD_DIM)

    for half in range(2):
        lanes = slice(half * HEAD_DIM, (half + 1) * HEAD_DIM)
        new_keys = spun(head(HEADS + group * 2 + half).astype(jnp.float32), cosine, sine).astype(jnp.bfloat16)
        new_values = head(HEADS + KV_HEADS + group * 2 + half)
        queries = [
            jnp.concatenate(
                [spun_ref[2 * STEPS * pair : 2 * STEPS * (pair + 1), columns(half, u)] for u in range(ratio)],
                axis=0,
            )
            for pair in range(pairs)
        ]
        old_scores = jnp.concatenate(
            [
                lax.dot_general(
                    queries[pair].astype(jnp.bfloat16),
                    keys_ref[2 * pair : 2 * pair + 2, :, lanes].reshape(2 * cached, HEAD_DIM),
                    contract_last,
                    preferred_element_type=jnp.float32,
                )
                for pair in range(pairs)
            ],
            axis=0,
        )
        new_scores = lax.dot_general(
            jnp.concatenate(queries, axis=0).astype(jnp.bfloat16),
            new_keys,
            contract_last,
            preferred_element_type=jnp.float32,
        )
        old_scores = jnp.where(old_kept, old_scores * scale, -1e30)
        new_scores = jnp.where(new_kept, new_scores * scale, -1e30)
        peak = jnp.maximum(
            jnp.max(old_scores, axis=1, keepdims=True), jnp.max(new_scores, axis=1, keepdims=True)
        )
        old_exp = jnp.exp(old_scores - peak)
        new_exp = jnp.exp(new_scores - peak)
        share = 1.0 / (jnp.sum(old_exp, axis=1, keepdims=True) + jnp.sum(new_exp, axis=1, keepdims=True))
        old_weights = old_exp * share
        fresh = jnp.dot(
            (new_exp * share).astype(jnp.bfloat16), new_values, preferred_element_type=jnp.float32
        )
        for pair in range(pairs):
            part = slice(pair * group_rows, (pair + 1) * group_rows)
            total = fresh[part] + jnp.dot(
                old_weights[part].astype(jnp.bfloat16),
                values_ref[2 * pair : 2 * pair + 2, :, lanes].reshape(2 * cached, HEAD_DIM),
                preferred_element_type=jnp.float32,
            )
            for u in range(ratio):
                sum_ref[2 * STEPS * pair : 2 * STEPS * (pair + 1), columns(half, u)] = total[
                    2 * STEPS * u : 2 * STEPS * (u + 1)
                ]
    out_ref[...] = sum_ref[...].astype(jnp.bfloat16)


def attend_slots(pieces, keys, values, lengths, rep_index):
    rows, cached = keys.shape[0], keys.shape[1]
    block_rows = 8
    tokens = block_rows * STEPS
    positions = (lengths[:, None] + jnp.arange(STEPS, dtype=jnp.int32)[None, :]).reshape(-1)
    frequency = jnp.power(
        jnp.float32(ROPE_BASE), -jnp.arange(0, HEAD_DIM, 2, dtype=jnp.float32) / HEAD_DIM
    )
    angles = positions.astype(jnp.float32)[:, None] * frequency[None, :]
    cosine, sine = jnp.cos(angles), jnp.sin(angles)
    cosine = jnp.concatenate([cosine, cosine], axis=1)
    sine = jnp.concatenate([-sine, sine], axis=1)
    width = QDIM // 4
    pair_width = KVD // 4
    return pl.pallas_call(
        attention_kernel,
        out_shape=jax.ShapeDtypeStruct((rows * STEPS, QDIM), jnp.bfloat16),
        grid_spec=pltpu.PrefetchScalarGridSpec(
            num_scalar_prefetch=2,
            grid=(rows // block_rows, 4),
            in_specs=[
                pl.BlockSpec((pieces.shape[0], tokens, pieces.shape[2]), lambda i, j, p, n: (0, i, 0)),
                pl.BlockSpec((tokens, HEAD_DIM), lambda i, j, p, n: (i, 0)),
                pl.BlockSpec((tokens, HEAD_DIM), lambda i, j, p, n: (i, 0)),
                pl.BlockSpec((block_rows, cached, pair_width), lambda i, j, p, n: (i, 0, p[0] ^ j)),
                pl.BlockSpec((block_rows, cached, pair_width), lambda i, j, p, n: (i, 0, p[0] ^ j)),
            ],
            out_specs=pl.BlockSpec((tokens, width), lambda i, j, p, n: (i, j)),
            scratch_shapes=[
                pltpu.VMEM((tokens, width), jnp.float32),
                pltpu.VMEM((tokens, width), jnp.float32),
            ],
        ),
        cost_estimate=pl.CostEstimate(flops=2_000_000_000, bytes_accessed=10_000_000, transcendentals=2_000_000),
        name="attend_slots",
    )(rep_index.astype(jnp.int32).reshape(1), lengths, pieces, cosine, sine, keys, values)


def product_kernel(blocks, groups, has_buffer, order_ref, *refs):
    refs = list(refs)
    row_refs = [refs.pop(0) for _ in range(blocks)]
    weight_refs = [refs.pop(0) for _ in range(4 * groups)]
    bias_ref = refs.pop(0)
    if has_buffer:
        refs.pop(0)
    out_ref, rows_vmem, weights_vmem, total, out_vmem, row_sem, weight_sem, out_sem = refs
    height = row_refs[0].shape[0]
    _, depth = weight_refs[0].shape

    def row_copy(m, j):
        columns = pl.ds(j * depth, depth) if isinstance(j, int) else pl.ds(pl.multiple_of(j * depth, depth), depth)
        return pltpu.make_async_copy(
            row_refs[m].at[:, columns],
            rows_vmem.at[pl.ds(m * height, height), columns],
            row_sem.at[m, j],
        )

    def weight_copy(i):
        return pltpu.make_async_copy(weight_refs[i], weights_vmem.at[i], weight_sem.at[i])

    for j in range(4):
        weight_copy(j).start()
        for m in range(blocks):
            row_copy(m, j).start()
    for i in range(4, 4 * groups):
        weight_copy(i).start()
    total[...] = jnp.zeros_like(total)

    @pl.loop(0, 4 * groups)
    def _(i):
        pltpu.make_async_copy(weight_refs[0], weights_vmem.at[i], weight_sem.at[i]).wait()

        @pl.when(i < 4)
        def _():
            for m in range(blocks):
                row_copy(m, i).wait()

        columns = pl.ds(pl.multiple_of(lax.rem(i, 4) * depth, depth), depth)
        total[i // 4] += lax.dot_general(
            rows_vmem[:, columns],
            weights_vmem[i],
            (((1,), (1,)), ((), ())),
            preferred_element_type=jnp.float32,
        )

    low_first = order_ref[blocks] == 1
    mine = total[0] + bias_ref[0:1]
    others = total[1] + bias_ref[1:2]

    @pl.when(low_first)
    def _():
        out_vmem[...] = jnp.concatenate([mine, others], axis=1).astype(jnp.bfloat16)

    @pl.when(jnp.logical_not(low_first))
    def _():
        out_vmem[...] = jnp.concatenate([others, mine], axis=1).astype(jnp.bfloat16)

    out_copies = [
        pltpu.make_async_copy(out_vmem.at[pl.ds(m * height, height)], out_ref.at[order_ref[m]], out_sem.at[m])
        for m in range(blocks)
    ]
    for copy in out_copies:
        copy.start()
    for copy in out_copies:
        copy.wait()


def product(row_blocks, weights, bias, order, buffer=None):
    blocks = len(row_blocks)
    groups = len(weights) // 4
    height, full = row_blocks[0].shape
    width, depth = weights[0].shape
    anywhere = pl.BlockSpec(memory_space=pl.ANY)
    inside = pl.BlockSpec(memory_space=pltpu.VMEM)
    operands = list(row_blocks) + list(weights) + [bias]
    specs = [anywhere] * (len(operands) - 1) + [inside]
    aliases = {}
    if buffer is not None:
        operands.append(buffer)
        specs.append(anywhere)
        aliases = {len(operands): 0}
    out_shape = jax.ShapeDtypeStruct((8, height, 2 * width), jnp.bfloat16)
    return pl.pallas_call(
        functools.partial(product_kernel, blocks, groups, buffer is not None),
        out_shape=out_shape,
        grid_spec=pltpu.PrefetchScalarGridSpec(
            num_scalar_prefetch=1,
            grid=(),
            in_specs=specs,
            out_specs=anywhere,
            scratch_shapes=[
                pltpu.VMEM((blocks * height, full), jnp.bfloat16),
                pltpu.VMEM((4 * groups, width, depth), jnp.bfloat16),
                pltpu.VMEM((groups, blocks * height, width), jnp.float32),
                pltpu.VMEM((blocks * height, 2 * width), jnp.bfloat16),
                pltpu.SemaphoreType.DMA((blocks, 4)),
                pltpu.SemaphoreType.DMA((4 * groups,)),
                pltpu.SemaphoreType.DMA((blocks,)),
            ],
        ),
        input_output_aliases=aliases,
        cost_estimate=pl.CostEstimate(
            flops=2 * blocks * height * full * width * groups,
            bytes_accessed=2 * full * width * groups + 2 * blocks * height * full,
            transcendentals=0,
        ),
        name="product",
    )(order, *operands)


def body(qkv_versions, qkv_bias, o_versions, norm_gain, hidden, cache_keys, cache_values, lengths):
    trainer_side = lax.axis_index("role") == 0
    shard_index = lax.axis_index("shard")
    rep_index = lax.axis_index("rep")
    rep_total = lax.axis_size("rep")
    own_qkv = qkv_versions[0].T
    own_out = o_versions[0]
    states = hidden[0].astype(jnp.float32)
    rows = states.shape[0]
    tokens = rows * STEPS
    near, far, low_first = owner_order(shard_index)
    normed = normalize(states, norm_gain[0]).reshape(tokens, D)
    qkv_slots = gather_weights(own_qkv)
    width = own_qkv.shape[0]
    bias = qkv_bias[0].astype(jnp.float32).reshape(1, -1)
    own_bias = lax.dynamic_slice_in_dim(bias, shard_index * width, width, 1)
    pair_bias = lax.dynamic_slice_in_dim(bias, (shard_index ^ 1) * width, width, 1)
    same, mirror = gather_rows(slot_columns(normed, rep_index))
    order = jnp.concatenate([near, far, low_first])
    spread = lax.all_to_all(own_out, "shard", split_axis=0, concat_axis=1, tiled=True)
    turned = rotate_columns(after(spread, same[3]))
    both_bias = jnp.concatenate([own_bias, pair_bias], axis=0)
    part = product(
        same + mirror, qkv_slots[0] + qkv_slots[1], both_bias, after(order, turned)
    )
    packed = to_owners(part)
    out_slots = gather_weights(after(own_out.T, turned), part, packed)
    weights = out_slots[0] + out_slots[1]
    folded_out = lax.all_to_all(
        after(turned, part), "shard", split_axis=1, concat_axis=0, tiled=True
    )
    sent_out = shifted(folded_out, "role", 1)
    packed = after(packed, out_slots[2], *weights[:6])
    attended = attend_slots(packed, cache_keys[0], cache_values[0], lengths[0], rep_index)
    folded_qkv = rotate_column_part(
        (after(qkv_slots[0][0], attended),) + qkv_slots[0][1:], rep_index, rep_total
    )
    sent_qkv = shifted(folded_qkv, "role", 1)
    same, mirror = gather_rows(attended)
    no_bias = jnp.zeros((2, own_out.shape[1]), jnp.float32)
    part = product(same, weights, no_bias, jnp.concatenate([near, low_first]))
    part = product(mirror, weights, no_bias, jnp.concatenate([far, low_first]), buffer=part)
    sent_qkv, sent_out = after(sent_qkv, part), after(sent_out, part)
    projected = to_owners(part)
    projected = projected.transpose(1, 0, 2).reshape(rows, STEPS, D).astype(jnp.float32)
    layer_out = (states + projected).astype(jnp.bfloat16)[None]
    new_qkv = jnp.where(trainer_side, folded_qkv, sent_qkv)
    new_o = jnp.where(trainer_side, folded_out, sent_out)
    return (layer_out, new_qkv.T[None], new_o[None])


def solution(mesh):
    in_specs = (
        P("role", "rep", "shard"),
        P("role", None),
        P("role", "rep", "shard"),
        P("role", None),
        P("role", ("shard", "rep"), None, None),
        P("role", ("shard", "rep"), None, None),
        P("role", ("shard", "rep"), None, None),
        P("role", ("shard", "rep")),
    )
    out_specs = (
        P("role", ("shard", "rep"), None, None),
        P("role", "rep", "shard"),
        P("role", "rep", "shard"),
    )
    return jax.shard_map(body, mesh=mesh, in_specs=in_specs, out_specs=out_specs, check_vma=False)
```
